32 devices in a mesh: wide: 8 (over y, x, core), narrow: 4 (over z).
Axes of the slice: x: 2, y: 2, z: 4, core: 2. Of those that a mesh axis runs over, the one named last changes fastest.
Arguments:
- cache: bfloat16 [8, 8192, 128], P('wide', 'narrow'), may hold values from -6 to 6
- lookup_slots: int32 [8, 4096, 16], P('wide'), may hold values from 0 to 8191
- bag_lengths: int32 [8, 4096], P('wide'), may hold values from 1 to 16
- miss_rows: bfloat16 [8, 4096, 128], P('wide', 'narrow'), may hold values from -6 to 6
- miss_slots: int32 [8, 4096], P('wide', 'narrow'), may hold values from 0 to 8191, as said below
- holder_counts: int32 [8, 16], P('wide', 'narrow'), may hold values from 0 to 512, as said below
- w_first: bfloat16 [1024, 4096], P(None, 'narrow'), may hold values from -0.1875 to 0.1875
- b_first: float32 [4096], P('narrow'), may hold values from -4 to 4
- w_second: bfloat16 [4096, 4096], P('narrow'), may hold values from -0.09375 to 0.09375
- b_second: float32 [4096], P('narrow'), may hold values from -4 to 4
- w_out: bfloat16 [4096], P('narrow'), may hold values from -0.09375 to 0.09375
Outputs:
- top_hidden: bfloat16 [4096, 4096], P('wide', 'narrow')
- logits: float32 [4096], P('wide')
- cache_next: bfloat16 [8, 8192, 128], P('wide', 'narrow')
The draws below stay inside these ranges and needn't reach their ends.
Inputs may be any that keep to these rules, and one draw needn't show every extreme that they name: `holder_counts`: entry h * 4 + o is the number of row blocks that holder h sections for owner o, the device holding slots o * 2048 to (o + 1) * 2048 - 1; a holder's counts sum to at most 1024, and this is reached by some holder of every table; the largest count, 512, is reached in every table. `miss_slots`: A holder's live entries are packed by owner, owner 0 first, as its counts say; each live entry names a slot of its owner, no slot twice in a table; entries past a holder's live ones are 0 and unused.
All inputs are finite; a program needn't handle non-finite values.
Results may differ from the reference program's by a relative error of at most 0.0076.
Values may be sent and summed in bfloat16 or wider, within the bound.
No kernel may reach another device: no remote copies, remote signals or barrier semaphores. Data moves between devices by JAX's collectives and lax.ppermute only.
A program may use at most 128 MiB of HBM per device.

```python
import math
import jax
import jax.numpy as jnp
import numpy as np
from jax import lax

EMB = 128
HID = 4096
BAG = 16
SLOT_DEV = 2048
SEND_CAP = 512
HOLD_CAP = 1024
F = 8
BATCH = 4096
SLOTS = 8192
N_NARROW = 4


def miss_plan(key):
    holder_count = N_NARROW
    keys = [jax.random.fold_in(key, 9100 + number) for number in range(4)]
    share = SEND_CAP // (holder_count - 1)
    excess = SEND_CAP - share * (holder_count - 1)
    owners = jnp.arange(holder_count, dtype=jnp.int32)[None, None, :]
    holders = jnp.arange(holder_count, dtype=jnp.int32)[None, :, None]
    base = jax.random.randint(keys[0], (F, holder_count, holder_count), 0, share + 1, dtype=jnp.int32)
    hottest = jax.random.randint(keys[1], (F, 1, 1), 0, holder_count, dtype=jnp.int32)
    fullest = jax.random.randint(keys[2], (F, 1, 1), 0, holder_count, dtype=jnp.int32)
    counts = jnp.where(owners == hottest, SEND_CAP, base)
    ranking = owners - (owners > hottest).astype(jnp.int32)
    filled = jnp.where(owners == hottest, SEND_CAP, share + jnp.where(ranking == 0, excess, 0))
    counts = jnp.where(holders == fullest, filled, counts).astype(jnp.int32)
    before = jnp.cumsum(counts, axis=1) - counts
    starts = jnp.cumsum(counts, axis=2) - counts
    totals = jnp.sum(counts, axis=2)
    bound = max(1, 2 ** 30 // SLOT_DEV)
    scores = jax.random.randint(keys[3], (F, holder_count, SLOT_DEV), 0, bound, dtype=jnp.int32) * SLOT_DEV
    scores = scores + jnp.arange(SLOT_DEV, dtype=jnp.int32)[None, None, :]
    orders = jnp.argsort(scores, axis=-1, stable=True).astype(jnp.int32)
    places = jnp.arange(HOLD_CAP, dtype=jnp.int32)[None, None, :]
    endings = starts + counts
    owner_of = jnp.sum((places[:, :, :, None] >= endings[:, :, None, :]).astype(jnp.int32), axis=3)
    owner_of = jnp.minimum(owner_of, holder_count - 1)
    first_place = jnp.take_along_axis(starts, owner_of, axis=2)
    offsets = jnp.take_along_axis(before, owner_of, axis=2)
    live = places < totals[:, :, None]
    columns = jnp.where(live, offsets + places - first_place, 0)
    columns = jnp.clip(columns, 0, SLOT_DEV - 1)
    flat_index = (owner_of * SLOT_DEV + columns).reshape(F, holder_count * HOLD_CAP)
    picked = jnp.take_along_axis(orders.reshape(F, holder_count * SLOT_DEV), flat_index, axis=1)
    slots = jnp.where(live, owner_of * SLOT_DEV + picked.reshape(F, holder_count, HOLD_CAP), 0)
    return (counts.reshape(F, holder_count * holder_count), slots.reshape(F, holder_count * HOLD_CAP).astype(jnp.int32))


def draw_holder_counts(key, part):
    return miss_plan(key)[0]


def draw_miss_slots(key, part):
    return miss_plan(key)[1]


def place_ends(values, key, smallest, high):
    place = [jax.random.randint(jax.random.fold_in(key, axis), (), 0, length) for axis, length in enumerate(values.shape)]
    longest = values.shape.index(max(values.shape))
    neighbour = place[:longest] + [(place[longest] + 1) % values.shape[longest]] + place[longest + 1:]
    return values.at[tuple(place)].set(smallest).at[tuple(neighbour)].set(high)


def shard_levels(key, extent, split, low, largest):
    level, own = 1.0, jax.random.fold_in(key, 6)
    for axis_at, shards_of in split:
        draws = jnp.exp(jax.random.uniform(jax.random.fold_in(own, axis_at), (shards_of,), jnp.float32, low / len(split), largest / len(split)))
        level = level * jnp.repeat(draws, extent[axis_at] // shards_of).reshape([-1 if axis == axis_at else 1 for axis in range(len(extent))])
    return level


def rank_bounds(amount, lean):
    loads = [(1 << 20) // math.isqrt(grade ** lean) + 1 for grade in range(1, amount + 1)]
    deviation = 1 + sum(loads) // (1 << 30)
    return np.cumsum(np.array([max(1, weight // deviation) for weight in loads]))


def skewed_ids(rng, extent, count, slope):
    listing = rank_bounds(count, slope)
    ticket = jax.random.randint(jax.random.fold_in(rng, 1), extent, 0, int(listing[count - 1]))
    grade = jnp.searchsorted(jnp.asarray(listing, jnp.int32), ticket, side="right")
    return jax.random.permutation(jax.random.fold_in(rng, 2), count)[grade].astype(jnp.int32)


def noise(rng, dims, deviation, limit, split=(), kind=jnp.bfloat16):
    loudness = shard_levels(rng, dims, split, -0.22, 0.18) if split else 1.0
    entries = jax.random.normal(rng, dims, jnp.float32) * deviation * loudness
    return jnp.minimum(jnp.maximum(entries, -limit), limit).astype(kind)


def setup_inputs(seed: int = 0) -> dict:
    seeds = jax.random.split(jax.random.key(seed), 12)
    return {
        "cache": noise(seeds[0], (F, SLOTS, EMB), 1.0, 6.0, ((0, 8), (1, 4))),
        "lookup_slots": place_ends(skewed_ids(seeds[1], (F, BATCH, BAG), SLOTS, 2), jax.random.fold_in(seeds[1], 3), 0, SLOTS - 1).astype(jnp.int32),
        "bag_lengths": place_ends(jax.random.randint(seeds[2], (F, BATCH), 1, BAG + 1), jax.random.fold_in(seeds[2], 1), 1, BAG).astype(jnp.int32),
        "miss_rows": noise(seeds[3], (F, N_NARROW * HOLD_CAP, EMB), 1.0, 6.0, ((0, 8), (1, 4))),
        "miss_slots": draw_miss_slots(jax.random.fold_in(seeds[11], 71), 0),
        "holder_counts": draw_holder_counts(jax.random.fold_in(seeds[11], 71), 0),
        "w_first": noise(seeds[6], (F * EMB, HID), (F * EMB) ** -0.5, 0.1875, ((1, 4),)),
        "b_first": noise(seeds[7], (HID,), 1.0, 4.0, ((0, 4),), jnp.float32),
        "w_second": noise(seeds[8], (HID, HID), HID ** -0.5, 0.09375, ((0, 4),)),
        "b_second": noise(seeds[9], (HID,), 1.0, 4.0, ((0, 4),), jnp.float32),
        "w_out": noise(seeds[10], (HID,), HID ** -0.5, 0.09375, ((0, 4),)),
    }


def reference(cache, lookup_slots, bag_lengths, miss_rows, miss_slots, holder_counts, w_first, b_first, w_second, b_second, w_out):
    table_count, batch_rows, bag_size = lookup_slots.shape
    emb_width = cache.shape[2]
    block_rows = math.gcd(batch_rows, 2048)
    block_count = batch_rows // block_rows
    usable = jnp.arange(bag_size, dtype=jnp.int32)[None, None, :] < bag_lengths[:, :, None]
    slot_blocks = lookup_slots.reshape(table_count * block_count, block_rows, bag_size)
    usable_blocks = usable.reshape(table_count * block_count, block_rows, bag_size)
    table_ids = jnp.repeat(jnp.arange(table_count, dtype=jnp.int32), block_count)

    def pool_block(member):
        table_id, positions, keep = member
        chosen = lax.dynamic_index_in_dim(cache, table_id, 0, keepdims=False)
        gathered = jnp.take(chosen, positions, axis=0).astype(jnp.float32)
        return jnp.sum(jnp.where(keep[..., None], gathered, jnp.zeros((), jnp.float32)), axis=1)

    pooled = lax.map(pool_block, (table_ids, slot_blocks, usable_blocks))
    pooled = pooled.reshape(table_count, batch_rows, emb_width).astype(jnp.bfloat16)
    features = jnp.transpose(pooled, (1, 0, 2)).reshape(batch_rows, table_count * emb_width)
    first_hidden = jnp.maximum(jnp.dot(features, w_first, preferred_element_type=jnp.float32) + b_first, 0.0).astype(jnp.bfloat16)
    top_hidden = jnp.maximum(jnp.dot(first_hidden, w_second, preferred_element_type=jnp.float32) + b_second, 0.0).astype(jnp.bfloat16)
    logits = jnp.dot(top_hidden, w_out, preferred_element_type=jnp.float32)

    holder_count = N_NARROW
    hold_rows = HOLD_CAP
    counts = holder_counts.reshape(table_count, holder_count, holder_count)
    totals = jnp.sum(counts, axis=2)
    live = jnp.arange(hold_rows, dtype=jnp.int32)[None, None, :] < totals[:, :, None]
    targets = jnp.where(live, miss_slots.reshape(table_count, holder_count, hold_rows), cache.shape[1])
    targets = targets.reshape(table_count, holder_count * hold_rows).astype(jnp.int32)

    def refill(chosen, target_rows, sectioned):
        return chosen.at[target_rows].set(sectioned, mode="drop")

    cache_next = jax.vmap(refill)(cache, targets, miss_rows)
    return top_hidden, logits, cache_next
```

```python
import jax
import jax.numpy as jnp
from jax import lax
from jax.experimental import pallas as pl
from jax.experimental.pallas import tpu as pltpu
from jax.sharding import PartitionSpec as P

SEND_CAP = 512
LOW = 256
GROUP = 16


def from_ahead(value, distance, count):
    pairs = [(source, (source - distance) % count) for source in range(count)]
    return lax.ppermute(value, "narrow", pairs)


def from_flipped(value, bit, count):
    return lax.ppermute(value, "wide", [(index, index ^ bit) for index in range(count)])


def pool_quarter(local_slots, cache_table, quarter):
    owners, quarters, blocks, width = local_slots.shape
    slot_count, emb = cache_table.shape
    highs = slot_count // LOW
    rows_per = blocks * GROUP
    total = owners * rows_per

    def kernel(quarter_ref, slots_ref, table_ref, out_ref, counts_ref):
        which = quarter_ref[0]
        key_rows = lax.broadcasted_iota(jnp.int32, (highs * GROUP, width), 0).astype(jnp.bfloat16)
        low_rows = lax.broadcasted_iota(jnp.int32, (LOW, width), 0).astype(jnp.bfloat16)
        bag_lane = lax.broadcasted_iota(jnp.int32, (blocks, width), 1) // (width // GROUP)
        one = jnp.ones((), jnp.bfloat16)
        zero = jnp.zeros((), jnp.bfloat16)

        def owner_step(owner, carry):
            slots = slots_ref[owner, which]
            keys = jnp.where(slots >= 0, (slots // LOW) * GROUP + bag_lane, -1)
            lows = slots & (LOW - 1)
            keys = keys.astype(jnp.float32).astype(jnp.bfloat16)
            lows = lows.astype(jnp.float32).astype(jnp.bfloat16)
            for block in range(blocks):
                hot_key = jnp.where(key_rows == keys[block : block + 1, :], one, zero)
                hot_low = jnp.where(low_rows == lows[block : block + 1, :], one, zero)
                counts = lax.dot_general(
                    hot_key, hot_low, (((1,), (1,)), ((), ())), preferred_element_type=jnp.float32
                )
                start = pl.multiple_of(owner * rows_per + block * GROUP, GROUP)
                counts_ref[:, pl.ds(start, GROUP), :] = counts.astype(jnp.bfloat16).reshape(
                    highs, GROUP, LOW
                )
            return carry

        lax.fori_loop(0, owners, owner_step, 0)
        tile = min(total, 512)

        def tile_step(index, carry):
            start = pl.multiple_of(index * tile, tile)
            acc = jnp.zeros((tile, emb), jnp.float32)
            for high in range(highs):
                acc = acc + jnp.dot(
                    counts_ref[high, pl.ds(start, tile), :],
                    table_ref[high * LOW : (high + 1) * LOW, :],
                    preferred_element_type=jnp.float32,
                )
            out_ref[pl.ds(start, tile), :] = acc.astype(jnp.bfloat16)
            return carry

        lax.fori_loop(0, total // tile, tile_step, 0)

    return pl.pallas_call(
        kernel,
        out_shape=jax.ShapeDtypeStruct((total, emb), jnp.bfloat16),
        in_specs=[
            pl.BlockSpec(memory_space=pltpu.SMEM),
            pl.BlockSpec(memory_space=pltpu.VMEM),
            pl.BlockSpec(memory_space=pltpu.VMEM),
        ],
        out_specs=pl.BlockSpec(memory_space=pltpu.VMEM),
        scratch_shapes=[pltpu.VMEM((highs, total, LOW), jnp.bfloat16)],
        cost_estimate=pl.CostEstimate(
            flops=4 * total * slot_count * emb, bytes_accessed=2 * total * emb, transcendentals=0
        ),
        name="pool_quarter",
    )(quarter.reshape(1), local_slots, cache_table)


def place_rows(targets, pieces, cache_table):
    slot_count, emb = cache_table.shape
    cap = pieces[0].shape[0]
    arrived = cap * len(pieces)
    tile = 256

    def kernel(targets_ref, *refs):
        piece_refs = refs[: len(pieces)]
        cache_ref, out_ref, rows_ref = refs[len(pieces) :]
        for index, piece in enumerate(piece_refs):
            rows_ref[index * cap : (index + 1) * cap, :emb] = piece[...]
        rows_ref[:, emb:] = jnp.ones((arrived, emb), jnp.bfloat16)
        lane_targets = targets_ref[...]

        def step(index, carry):
            start = pl.multiple_of(index * tile, tile)
            slot_rows = lax.broadcasted_iota(jnp.int32, (tile, arrived), 0) + start
            hot = jnp.where(slot_rows == lane_targets, 1.0, 0.0).astype(jnp.bfloat16)
            placed = jnp.dot(hot, rows_ref[...], preferred_element_type=jnp.float32)
            old = cache_ref[pl.ds(start, tile), :]
            fresh = jnp.where(placed[:, emb:] > 0.5, placed[:, :emb], old.astype(jnp.float32))
            out_ref[pl.ds(start, tile), :] = fresh.astype(jnp.bfloat16)
            return carry

        lax.fori_loop(0, slot_count // tile, step, 0)

    return pl.pallas_call(
        kernel,
        out_shape=jax.ShapeDtypeStruct((slot_count, emb), jnp.bfloat16),
        scratch_shapes=[pltpu.VMEM((arrived, 2 * emb), jnp.bfloat16)],
        cost_estimate=pl.CostEstimate(
            flops=4 * arrived * slot_count * emb,
            bytes_accessed=4 * slot_count * emb,
            transcendentals=0,
        ),
        name="place_rows",
    )(targets.reshape(1, arrived), *pieces, cache_table)


def top_network(features, first_own, second_own, first_parts, second_parts, biases, b_second, w_out):
    count = len(features)
    quarter_rows, depth = features[0].shape
    rows = count * quarter_rows
    hidden = first_own.shape[1]
    columns = second_own.shape[1] // count
    flat_parts, layout = [], []
    for which, family in enumerate((first_parts, second_parts)):
        for distance, parts in enumerate(family, start=1):
            for masks, array in parts:
                layout.append((which, distance, masks, array.shape[0] // len(masks)))
                flat_parts.append(array)
    tile = 256

    def kernel(*refs):
        feature_refs = refs[:count]
        first_ref, second_ref = refs[count : count + 2]
        part_refs = refs[count + 2 : count + 2 + len(flat_parts)]
        rest = refs[count + 2 + len(flat_parts) :]
        bias_ref, b_second_ref, w_out_ref, top_ref, logit_ref = rest[:5]
        feats, firsts, seconds, hiddens, feat_sem, sems = rest[5:]
        wide_index = lax.axis_index("wide")
        narrow_index = lax.axis_index("narrow")
        copies = []
        for distance, ref in enumerate(feature_refs):
            spot = lax.rem(narrow_index + distance, count) * quarter_rows
            spot = pl.multiple_of(spot, quarter_rows)
            pltpu.make_async_copy(ref, feats.at[pl.ds(spot, quarter_rows), :], feat_sem).start()
        pltpu.make_async_copy(first_ref, firsts.at[0], sems.at[0, 0]).start()
        column = pl.multiple_of(narrow_index * columns, columns)
        own_second = pltpu.make_async_copy(
            second_ref.at[:, pl.ds(column, columns)], seconds.at[0], sems.at[1, 0]
        )
        for wanted in (0, 1):
            for (which, distance, masks, height), ref in zip(layout, part_refs):
                if which != wanted:
                    continue
                target = firsts if which == 0 else seconds
                for position, mask in enumerate(masks):
                    spot = pl.multiple_of((wide_index ^ mask) * height, height)
                    pltpu.make_async_copy(
                        ref.at[position * height : (position + 1) * height, :],
                        target.at[distance, pl.ds(spot, height), :],
                        sems.at[which, distance],
                    ).start()
            if wanted == 0:
                own_second.start()
        pltpu.make_async_copy(feats, feats, feat_sem).wait()
        for distance in range(count):
            pltpu.make_async_copy(firsts.at[distance], firsts.at[distance], sems.at[0, distance]).wait()

            def first_step(index, carry):
                start = pl.multiple_of(index * tile, tile)
                terms = jnp.dot(
                    feats[...],
                    firsts[distance, :, pl.ds(start, tile)],
                    preferred_element_type=jnp.float32,
                )
                terms = jnp.maximum(terms + bias_ref[distance : distance + 1, pl.ds(start, tile)], 0.0)
                spot = pl.multiple_of(distance * hidden + start, tile)
                hiddens[:, pl.ds(spot, tile)] = terms.astype(jnp.bfloat16)
                return carry

            lax.fori_loop(0, hidden // tile, first_step, 0)
        for distance in range(count):
            pltpu.make_async_copy(
                seconds.at[distance], seconds.at[distance], sems.at[1, distance]
            ).wait()

        def second_step(index, carry):
            start = pl.multiple_of(index * tile, tile)
            terms = jnp.zeros((rows, tile), jnp.float32)
            for distance in range(count):
                terms = terms + jnp.dot(
                    hiddens[:, distance * hidden : (distance + 1) * hidden],
                    seconds[distance, :, pl.ds(start, tile)],
                    preferred_element_type=jnp.float32,
                )
            terms = jnp.maximum(terms + b_second_ref[:, pl.ds(start, tile)], 0.0)
            top_ref[:, pl.ds(start, tile)] = terms.astype(jnp.bfloat16)
            return carry

        lax.fori_loop(0, columns // tile, second_step, 0)
        logit_ref[...] = lax.dot_general(
            w_out_ref[...], top_ref[...], (((1,), (1,)), ((), ())), preferred_element_type=jnp.float32
        )

    anywhere = pl.BlockSpec(memory_space=pl.ANY)
    local = pl.BlockSpec(memory_space=pltpu.VMEM)
    return pl.pallas_call(
        kernel,
        out_shape=(
            jax.ShapeDtypeStruct((rows, columns), jnp.bfloat16),
            jax.ShapeDtypeStruct((8, rows), jnp.float32),
        ),
        in_specs=[anywhere] * (count + 2 + len(flat_parts)) + [local] * 3,
        out_specs=(local, local),
        scratch_shapes=[
            pltpu.VMEM((rows, depth), jnp.bfloat16),
            pltpu.VMEM((count, depth, hidden), jnp.bfloat16),
            pltpu.VMEM((count, hidden, columns), jnp.bfloat16),
            pltpu.VMEM((rows, count * hidden), jnp.bfloat16),
            pltpu.SemaphoreType.DMA,
            pltpu.SemaphoreType.DMA((2, count)),
        ],
        cost_estimate=pl.CostEstimate(
            flops=2 * rows * count * hidden * (depth + columns),
            bytes_accessed=2 * count * hidden * (depth + columns),
            transcendentals=0,
        ),
        name="top_network",
    )(
        *features,
        first_own,
        second_own,
        *flat_parts,
        jnp.stack(biases),
        b_second.reshape(1, columns),
        jnp.broadcast_to(w_out.reshape(1, columns), (8, columns)),
    )


def spread(piece, bits, wide_count):
    pieces = [([0], piece)]
    for bit in bits:
        masks = [mask for held, _ in pieces for mask in held]
        arrays = [array for _, array in pieces]
        message = arrays[0] if len(arrays) == 1 else jnp.concatenate(arrays, axis=0)
        pieces.append(([mask ^ bit for mask in masks], from_flipped(message, bit, wide_count)))
    for masks, array in list(pieces):
        pieces.append(([mask ^ 1 for mask in masks], from_flipped(array, 1, wide_count)))
    return pieces


def body(
    cache,
    lookup_slots,
    bag_lengths,
    miss_rows,
    miss_slots,
    holder_counts,
    w_first,
    b_first,
    w_second,
    b_second,
    w_out,
):
    wide_count = lax.axis_size("wide")
    count = lax.axis_size("narrow")
    wide_index = lax.axis_index("wide")
    narrow_index = lax.axis_index("narrow")
    cache_table = cache[0]
    slot_count, emb = cache_table.shape
    lookups = lookup_slots[0]
    lengths = bag_lengths[0]
    batch_rows, bag_size = lookups.shape
    owner_rows = batch_rows // wide_count
    quarter_rows = owner_rows // count
    columns = w_second.shape[1] // count

    bits = [1 << place for place in range(1, (wide_count - 1).bit_length())]
    first_height = w_first.shape[0] // wide_count
    second_height = w_second.shape[0] // wide_count
    first_slice = lax.dynamic_slice_in_dim(w_first, wide_index * first_height, first_height, 0)
    biases, first_parts, second_parts = [b_first], [], []
    for distance in range(1, count):
        taker = lax.rem(narrow_index + count - distance, count)
        second_slice = lax.dynamic_slice(
            w_second,
            (wide_index * second_height, taker * columns),
            (second_height, columns),
        )
        biases.append(from_ahead(b_first, distance, count))
        first_parts.append(spread(from_ahead(first_slice, distance, count), bits, wide_count))
        second_parts.append(
            spread(from_ahead(second_slice, distance, count), bits[::-1], wide_count)
        )

    local_slots = lookups - narrow_index * slot_count
    usable = jnp.arange(bag_size, dtype=jnp.int32)[None, :] < lengths[:, None]
    usable = usable & (local_slots >= 0) & (local_slots < slot_count)
    local_slots = jnp.where(usable, local_slots, -1).reshape(
        wide_count, count, quarter_rows // GROUP, GROUP * bag_size
    )
    summed = None
    for distance in range(count - 1, -1, -1):
        taker = lax.rem(narrow_index + count - distance, count)
        part = pool_quarter(local_slots, cache_table, taker)
        if distance:
            part = from_ahead(part, distance, count)
        part = part.astype(jnp.float32)
        summed = part if summed is None else summed + part
    summed = summed.astype(jnp.bfloat16).reshape(wide_count, quarter_rows, emb)
    arrived = lax.all_to_all(summed, "wide", split_axis=0, concat_axis=0, tiled=True)
    own_features = jnp.transpose(arrived, (1, 0, 2)).reshape(quarter_rows, wide_count * emb)
    features = [own_features] + [
        from_ahead(own_features, distance, count) for distance in range(1, count)
    ]

    top_hidden, logit_terms = top_network(
        features, w_first, w_second, first_parts, second_parts, biases, b_second, w_out
    )
    own_terms = logit_terms[0:1]
    gathered = jnp.zeros((count, owner_rows), jnp.float32)
    for distance in range(count):
        terms = from_ahead(own_terms, distance, count) if distance else own_terms
        spot = lax.rem(narrow_index + distance, count)
        gathered = lax.dynamic_update_slice_in_dim(gathered, terms, spot, 0)
    logits = jnp.sum(gathered, axis=0)

    counts = holder_counts[0]
    starts = jnp.cumsum(counts) - counts
    padded_rows = jnp.concatenate([miss_rows[0], jnp.zeros((SEND_CAP, emb), miss_rows.dtype)])
    padded_slots = jnp.concatenate([miss_slots[0], jnp.zeros((SEND_CAP,), jnp.int32)])
    column_ids = jnp.arange(SEND_CAP, dtype=jnp.int32)
    got_rows, got_slots = [], []
    for distance in range(count):
        owner = lax.rem(narrow_index + count - distance, count)
        start = starts[owner]
        rows = lax.dynamic_slice(padded_rows, (start, 0), (SEND_CAP, emb))
        slots = lax.dynamic_slice(padded_slots, (start,), (SEND_CAP,))
        slots = jnp.where(column_ids < counts[owner], slots - owner * slot_count, -1)
        if distance:
            rows = from_ahead(rows, distance, count)
            slots = from_ahead(slots, distance, count)
        got_rows.append(rows)
        got_slots.append(slots)
    cache_next = place_rows(jnp.concatenate(got_slots), got_rows, cache_table)[None]
    return (top_hidden, logits, cache_next)


def solution(mesh):
    return jax.shard_map(
        body,
        mesh=mesh,
        in_specs=(
            P("wide", "narrow", None),
            P("wide", None, None),
            P("wide", None),
            P("wide", "narrow", None),
            P("wide", "narrow"),
            P("wide", "narrow"),
            P(None, "narrow"),
            P("narrow"),
            P("narrow", None),
            P("narrow"),
            P("narrow"),
        ),
        out_specs=(P("wide", "narrow"), P("wide"), P("wide", "narrow", None)),
        check_vma=False,
    )
```

```python
import jax
import jax.numpy as jnp
from jax import lax
from jax.experimental import pallas as pl
from jax.experimental.pallas import tpu as pltpu
from jax.sharding import PartitionSpec as P


SEND_CAP = 512
LOW_BITS = 8
LOW = 1 << LOW_BITS
GROUP = 16


def from_ahead(value, distance, count):
    pairs = [(source, (source - distance) % count) for source in range(count)]
    return lax.ppermute(value, "narrow", pairs)


def from_flipped(value, bit, count):
    return lax.ppermute(value, "wide", [(index, index ^ bit) for index in range(count)])


def pool_quarter(lookups, lengths, cache_table, distance):
    owners, quarters, blocks, width = lookups.shape
    slot_count, emb = cache_table.shape
    highs = slot_count // LOW
    rows_per = blocks * GROUP
    total = owners * rows_per

    def kernel(lookups_ref, lengths_ref, table_ref, out_ref, counts_ref):
        here = lax.axis_index("narrow")
        which = lax.rem(here + quarters - distance, quarters)
        base = here * slot_count
        bag_size = width // GROUP
        key_rows = lax.broadcasted_iota(jnp.int32, (highs * GROUP, width), 0).astype(jnp.bfloat16)
        low_rows = lax.broadcasted_iota(jnp.int32, (LOW, width), 0).astype(jnp.bfloat16)
        lane = lax.broadcasted_iota(jnp.int32, (blocks, width), 1)
        bag_lane = lane // bag_size
        place_lane = lane - bag_lane * bag_size
        bag_rows = lax.broadcasted_iota(jnp.int32, (rows_per, width), 0) & (GROUP - 1)
        bag_lanes = lax.broadcasted_iota(jnp.int32, (rows_per, width), 1) // bag_size
        widen = jnp.where(bag_rows == bag_lanes, 1.0, 0.0).astype(jnp.bfloat16)
        row_block = lax.broadcasted_iota(jnp.int32, (blocks, rows_per), 1) // GROUP
        own_block = row_block == lax.broadcasted_iota(jnp.int32, (blocks, rows_per), 0)
        one = jnp.ones((), jnp.bfloat16)
        zero = jnp.zeros((), jnp.bfloat16)

        def owner_step(owner, carry):
            slots = lookups_ref[owner, which] - base
            bag_lengths = lengths_ref[pl.ds(owner * quarters + which, 1), :].astype(jnp.float32)
            bag_lengths = jnp.where(own_block, bag_lengths, 0.0).astype(jnp.bfloat16)
            used = jnp.dot(bag_lengths, widen, preferred_element_type=jnp.float32)
            used = used.astype(jnp.int32)
            usable = (place_lane < used) & (slots >= 0) & (slots < slot_count)
            keys = jnp.where(usable, (slots >> LOW_BITS) * GROUP + bag_lane, -1)
            lows = slots & (LOW - 1)
            keys = keys.astype(jnp.float32).astype(jnp.bfloat16)
            lows = lows.astype(jnp.float32).astype(jnp.bfloat16)
            for block in range(blocks):
                hot_key = jnp.where(key_rows == keys[block : block + 1, :], one, zero)
                hot_low = jnp.where(low_rows == lows[block : block + 1, :], one, zero)
                counts = lax.dot_general(
                    hot_key.astype(jnp.float8_e4m3fn),
                    hot_low.astype(jnp.float8_e4m3fn),
                    (((1,), (1,)), ((), ())),
                    preferred_element_type=jnp.float32,
                )
                start = pl.multiple_of(owner * rows_per + block * GROUP, GROUP)
                counts_ref[:, pl.ds(start, GROUP), :] = counts.astype(jnp.bfloat16).reshape(
                    highs, GROUP, LOW
                )
            return carry

        lax.fori_loop(0, owners, owner_step, 0, unroll=2)
        tile = min(total, 512)

        def tile_step(index, carry):
            start = pl.multiple_of(index * tile, tile)
            acc = jnp.zeros((tile, emb), jnp.float32)
            for high in range(highs):
                acc = acc + jnp.dot(
                    counts_ref[high, pl.ds(start, tile), :],
                    table_ref[high * LOW : (high + 1) * LOW, :],
                    preferred_element_type=jnp.float32,
                )
            out_ref[pl.ds(start, tile), :] = acc.astype(jnp.bfloat16)
            return carry

        lax.fori_loop(0, total // tile, tile_step, 0)

    return pl.pallas_call(
        kernel,
        out_shape=jax.ShapeDtypeStruct((total, emb), jnp.bfloat16),
        scratch_shapes=[pltpu.VMEM((highs, total, LOW), jnp.bfloat16)],
        cost_estimate=pl.CostEstimate(
            flops=4 * total * slot_count * emb, bytes_accessed=2 * total * emb, transcendentals=0
        ),
        name="pool_quarter",
    )(lookups, lengths, cache_table)


def section_rows(counts, rows, slots, slot_count):
    count = counts.shape[0]
    held, emb = rows.shape
    spans = SEND_CAP // emb

    def kernel(counts_ref, rows_ref, slots_ref, *out_refs):
        here = lax.axis_index("narrow")
        row_ids = lax.broadcasted_iota(jnp.int32, (SEND_CAP, held), 0)
        places = lax.broadcasted_iota(jnp.int32, (SEND_CAP, held), 1)
        live_lanes = lax.broadcasted_iota(jnp.int32, (1, SEND_CAP), 1)
        for distance, out_ref in enumerate(out_refs):
            owner = lax.rem(here + count - distance, count)
            start = jnp.int32(0)
            for other in range(count):
                start = start + jnp.where(other < owner, counts_ref[other], 0)
            live = counts_ref[owner]
            source = jnp.where(row_ids < live, row_ids + start, -1)
            hot = jnp.where(source == places, 1.0, 0.0).astype(jnp.bfloat16)
            picked = jnp.dot(hot, rows_ref[...], preferred_element_type=jnp.float32)
            out_ref[:SEND_CAP, :] = picked.astype(jnp.bfloat16)
            local = slots_ref[...] - owner * slot_count
            digits = jnp.concatenate([local >> LOW_BITS, local & (LOW - 1)] * 4, axis=0)
            digits = digits.astype(jnp.float32).astype(jnp.bfloat16)
            moved = lax.dot_general(
                digits, hot, (((1,), (1,)), ((), ())), preferred_element_type=jnp.float32
            )
            high = jnp.where(live_lanes < live, moved[0:1, :], -1.0)
            low = moved[1:2, :]
            tail = [high[:, span * emb : (span + 1) * emb] for span in range(spans)]
            tail += [low[:, span * emb : (span + 1) * emb] for span in range(spans)]
            tail.append(jnp.zeros((GROUP - 2 * spans, emb), jnp.float32))
            out_ref[SEND_CAP:, :] = jnp.concatenate(tail, axis=0).astype(jnp.bfloat16)

    smem = pl.BlockSpec(memory_space=pltpu.SMEM)
    vmem = pl.BlockSpec(memory_space=pltpu.VMEM)
    return pl.pallas_call(
        kernel,
        out_shape=tuple(
            jax.ShapeDtypeStruct((SEND_CAP + GROUP, emb), jnp.bfloat16) for _ in range(count)
        ),
        in_specs=[smem, vmem, vmem],
        out_specs=tuple(vmem for _ in range(count)),
        cost_estimate=pl.CostEstimate(
            flops=2 * count * SEND_CAP * held * emb,
            bytes_accessed=4 * held * emb,
            transcendentals=0,
        ),
        name="section_rows",
    )(counts, rows, slots.reshape(1, held))


def place_rows(pieces, cache_table):
    slot_count, emb = cache_table.shape
    spans = SEND_CAP // emb
    arrived = SEND_CAP * len(pieces)

    def kernel(*refs):
        piece_refs = refs[: len(pieces)]
        cache_ref, out_ref, rows_ref = refs[len(pieces) :]
        high, low = [], []
        for index, piece in enumerate(piece_refs):
            rows_ref[index * SEND_CAP : (index + 1) * SEND_CAP, :emb] = piece[:SEND_CAP, :]
            digits = piece[SEND_CAP:, :].astype(jnp.float32)
            high += [digits[span : span + 1, :] for span in range(spans)]
            low += [digits[spans + span : spans + span + 1, :] for span in range(spans)]
        rows_ref[:, emb:] = jnp.ones((arrived, emb), jnp.bfloat16)
        high = jnp.concatenate(high, axis=1)
        low = jnp.concatenate(low, axis=1)
        low_rows = lax.broadcasted_iota(jnp.int32, (LOW, arrived), 0).astype(jnp.bfloat16)
        one = jnp.ones((), jnp.bfloat16)
        zero = jnp.zeros((), jnp.bfloat16)

        def step(index, carry):
            start = pl.multiple_of(index * LOW, LOW)
            targets = jnp.where(high == index.astype(jnp.float32), low, -1.0).astype(jnp.bfloat16)
            hot = jnp.where(low_rows == targets, one, zero)
            placed = jnp.dot(hot, rows_ref[...], preferred_element_type=jnp.float32)
            old = cache_ref[pl.ds(start, LOW), :]
            fresh = jnp.where(placed[:, emb:] > 0.5, placed[:, :emb], old.astype(jnp.float32))
            out_ref[pl.ds(start, LOW), :] = fresh.astype(jnp.bfloat16)
            return carry

        lax.fori_loop(0, slot_count // LOW, step, 0, unroll=2)

    return pl.pallas_call(
        kernel,
        out_shape=jax.ShapeDtypeStruct((slot_count, emb), jnp.bfloat16),
        scratch_shapes=[pltpu.VMEM((arrived, 2 * emb), jnp.bfloat16)],
        cost_estimate=pl.CostEstimate(
            flops=4 * arrived * slot_count * emb,
            bytes_accessed=4 * slot_count * emb,
            transcendentals=0,
        ),
        name="place_rows",
    )(*pieces, cache_table)


def top_network(features, first_own, second_own, parts, biases, b_second, w_out):
    count = len(features)
    quarter_rows, depth = features[0].shape
    rows = count * quarter_rows
    hidden = first_own.shape[1]
    columns = second_own.shape[1] // count
    flat_parts, layout = [], []
    for distance, pieces in parts.items():
        for mask, array, spans in pieces:
            layout.append((distance, mask, spans))
            flat_parts.append(array)
    tile = min(hidden, 512)

    def kernel(*refs):
        feature_refs = refs[:count]
        first_ref, second_ref = refs[count : count + 2]
        part_refs = refs[count + 2 : count + 2 + len(flat_parts)]
        rest = refs[count + 2 + len(flat_parts) :]
        bias_ref, b_second_ref, w_out_ref, top_ref, logit_ref = rest[:5]
        feats, firsts, seconds, hiddens, feat_sem, sems = rest[5:]
        wide_index = lax.axis_index("wide")
        narrow_index = lax.axis_index("narrow")
        for distance, ref in enumerate(feature_refs):
            spot = lax.rem(narrow_index + distance, count) * quarter_rows
            spot = pl.multiple_of(spot, quarter_rows)
            pltpu.make_async_copy(ref, feats.at[pl.ds(spot, quarter_rows), :], feat_sem).start()
        column = pl.multiple_of(narrow_index * columns, columns)

        def fetch(which, wanted):
            if wanted == 0:
                if which == 0:
                    source, target = first_ref, firsts.at[0]
                else:
                    source = second_ref.at[:, pl.ds(column, columns)]
                    target = seconds.at[:hidden, :]
                pltpu.make_async_copy(source, target, sems.at[which, 0]).start()
            for (distance, mask, spans), ref in zip(layout, part_refs):
                for layer, row, height in spans:
                    if layer != which or distance != wanted:
                        continue
                    spot = pl.multiple_of((wide_index ^ mask) * height, height)
                    target = firsts.at[distance] if which == 0 else seconds
                    spot = spot + which * distance * hidden
                    pltpu.make_async_copy(
                        ref.at[row : row + height, :],
                        target.at[pl.ds(spot, height), :],
                        sems.at[which, distance],
                    ).start()

        for distance in range(count):
            fetch(0, distance)
        pltpu.make_async_copy(feats, feats, feat_sem).wait()
        for distance in range(count):
            pltpu.make_async_copy(firsts.at[distance], firsts.at[distance], sems.at[0, distance]).wait()
            fetch(1, distance)
            for start in range(0, hidden, tile):
                terms = jnp.dot(
                    feats[...],
                    firsts[distance, :, start : start + tile],
                    preferred_element_type=jnp.float32,
                )
                bias = bias_ref[distance : distance + 1, start : start + tile]
                spot = distance * hidden + start
                hiddens[:, spot : spot + tile] = jnp.maximum(terms + bias, 0.0).astype(jnp.bfloat16)
        for distance in range(count):
            block = seconds.at[distance * hidden : (distance + 1) * hidden, :]
            pltpu.make_async_copy(block, block, sems.at[1, distance]).wait()
        for start in range(0, columns, tile):
            terms = jnp.dot(
                hiddens[...], seconds[:, start : start + tile], preferred_element_type=jnp.float32
            )
            terms = jnp.maximum(terms + b_second_ref[:, start : start + tile], 0.0)
            top_ref[:, start : start + tile] = terms.astype(jnp.bfloat16)
        logit_ref[...] = lax.dot_general(
            w_out_ref[...], top_ref[...], (((1,), (1,)), ((), ())), preferred_element_type=jnp.float32
        )[:1]

    anywhere = pl.BlockSpec(memory_space=pl.ANY)
    local = pl.BlockSpec(memory_space=pltpu.VMEM)
    return pl.pallas_call(
        kernel,
        out_shape=(
            jax.ShapeDtypeStruct((rows, columns), jnp.bfloat16),
            jax.ShapeDtypeStruct((1, rows), jnp.float32),
        ),
        in_specs=[anywhere] * (count + 2 + len(flat_parts)) + [local] * 3,
        out_specs=(local, local),
        scratch_shapes=[
            pltpu.VMEM((rows, depth), jnp.bfloat16),
            pltpu.VMEM((count, depth, hidden), jnp.bfloat16),
            pltpu.VMEM((count * hidden, columns), jnp.bfloat16),
            pltpu.VMEM((rows, count * hidden), jnp.bfloat16),
            pltpu.SemaphoreType.DMA,
            pltpu.SemaphoreType.DMA((2, count)),
        ],
        cost_estimate=pl.CostEstimate(
            flops=2 * rows * count * hidden * (depth + columns),
            bytes_accessed=2 * count * hidden * (depth + columns),
            transcendentals=0,
        ),
        name="top_network",
    )(
        *features,
        first_own,
        second_own,
        *flat_parts,
        jnp.stack(biases),
        b_second.reshape(1, columns),
        jnp.broadcast_to(w_out.reshape(1, columns), (8, columns)),
    )


def after(value, *earlier):
    return lax.optimization_barrier((value,) + earlier)[0]


def spread(piece, spans, bits, wide_count, gate=None):
    if gate is not None:
        piece = after(piece, gate)
    pieces = [(0, piece)]
    for bit in bits:
        pieces = pieces + [
            (mask ^ bit, from_flipped(array, bit, wide_count)) for mask, array in pieces
        ]
    pieces = pieces + [
        (mask ^ 1, from_flipped(array, 1, wide_count)) for mask, array in pieces
    ]
    return [(mask, array, spans) for mask, array in pieces]


def step(
    cache,
    lookup_slots,
    bag_lengths,
    miss_rows,
    miss_slots,
    holder_counts,
    w_first,
    b_first,
    w_second,
    b_second,
    w_out,
):
    wide_count = lax.axis_size("wide")
    count = lax.axis_size("narrow")
    wide_index = lax.axis_index("wide")
    narrow_index = lax.axis_index("narrow")
    cache_table = cache[0]
    slot_count, emb = cache_table.shape
    lookups = lookup_slots[0]
    lengths = bag_lengths[0]
    batch_rows, bag_size = lookups.shape
    owner_rows = batch_rows // wide_count
    quarter_rows = owner_rows // count
    columns = w_second.shape[1] // count

    bits = [1 << place for place in range(1, (wide_count - 1).bit_length())]
    first_height = w_first.shape[0] // wide_count
    second_height = w_second.shape[0] // wide_count
    first_slice = lax.dynamic_slice_in_dim(w_first, wide_index * first_height, first_height, 0)

    def slices_for(distance):
        taker = lax.rem(narrow_index + count - distance, count)
        second_slice = lax.dynamic_slice(
            w_second,
            (wide_index * second_height, taker * columns),
            (second_height, columns),
        )
        return first_slice, second_slice

    both_spans = ((0, 0, first_height), (1, first_height, second_height))

    def merged(distance, gate=None):
        message = jnp.concatenate(slices_for(distance), axis=0)
        if gate is not None:
            message = after(message, gate)
        return from_ahead(message, distance, count)

    last = count - 1
    arrived_slices = {distance: merged(distance) for distance in range(1, last)}

    lookups = lookups.reshape(wide_count, count, quarter_rows // GROUP, GROUP * bag_size)
    lengths = lengths.reshape(wide_count * count, quarter_rows)
    sent, pooled = [], []
    for distance in range(count - 1, -1, -1):
        own_part = pool_quarter(lookups, lengths, cache_table, distance)
        pooled.append(own_part)
        if distance:
            sent.append(from_ahead(own_part, distance, count))
    biases = [b_first]
    for distance in range(1, count):
        biases.append(from_ahead(after(b_first, own_part), distance, count))
    summed = own_part.astype(jnp.float32)
    for part in sent:
        summed = summed + part.astype(jnp.float32)
    summed = summed.astype(jnp.bfloat16).reshape(wide_count, quarter_rows, emb)
    arrived_slices[last] = [
        from_ahead(after(piece, summed), last, count) for piece in slices_for(last)
    ]
    arrived = lax.all_to_all(summed, "wide", split_axis=0, concat_axis=0, tiled=True)
    own_features = jnp.transpose(arrived, (1, 0, 2)).reshape(quarter_rows, wide_count * emb)
    features = [own_features] + [
        from_ahead(own_features, distance, count) for distance in range(1, count)
    ]

    sections = section_rows(
        holder_counts[0], after(miss_rows[0], own_features), miss_slots[0], slot_count
    )
    arrived_rows = [sections[0]] + [
        from_ahead(sections[distance], distance, count) for distance in range(1, count)
    ]

    parts = {}
    for distance in range(1, last):
        ordered = bits if distance % 2 else bits[::-1]
        parts[distance] = spread(
            arrived_slices[distance],
            both_spans,
            ordered,
            wide_count,
            pooled[min(2 * distance - 1, last)],
        )
    first_piece, second_piece = arrived_slices[last]
    parts[last] = spread(
        first_piece, ((0, 0, first_height),), bits, wide_count, own_features
    ) + spread(second_piece, ((1, 0, second_height),), bits[::-1], wide_count, own_features)
    top_hidden, logit_terms = top_network(
        features, w_first, w_second, parts, biases, b_second, w_out
    )
    shares = [logit_terms] + [
        from_ahead(logit_terms, distance, count) for distance in range(1, count)
    ]
    while len(shares) > 1:
        half = len(shares) // 2
        shares = [shares[place] + shares[place + half] for place in range(half)]
    logits = shares[0].reshape(owner_rows)

    cache_next = place_rows(arrived_rows, cache_table)[None]
    return (top_hidden, logits, cache_next)


def solution(mesh):
    return jax.shard_map(
        step,
        mesh=mesh,
        in_specs=(
            P("wide", "narrow", None),
            P("wide", None, None),
            P("wide", None),
            P("wide", "narrow", None),
            P("wide", "narrow"),
            P("wide", "narrow"),
            P(None, "narrow"),
            P("narrow"),
            P("narrow", None),
            P("narrow"),
            P("narrow"),
        ),
        out_specs=(P("wide", "narrow"), P("wide"), P("wide", "narrow", None)),
        check_vma=False,
    )
```

```python
import jax
import jax.numpy as jnp
from jax import lax
from jax.experimental import pallas as pl
from jax.experimental.pallas import tpu as pltpu
from jax.sharding import PartitionSpec as P


SEND_CAP = 512
LOW_BITS = 8
LOW = 1 << LOW_BITS
GROUP = 16


def from_ahead(value, distance, count):
    pairs = [(source, (source - distance) % count) for source in range(count)]
    return lax.ppermute(value, "narrow", pairs)


def from_flipped(value, bit, count):
    return lax.ppermute(value, "wide", [(index, index ^ bit) for index in range(count)])


def pool_quarter(lookups, lengths, cache_table, distance):
    owners, quarters, blocks, width = lookups.shape
    slot_count, emb = cache_table.shape
    highs = slot_count // LOW
    rows_per = blocks * GROUP
    total = owners * rows_per

    def kernel(lookups_ref, lengths_ref, table_ref, out_ref, counts_ref):
        here = lax.axis_index("narrow")
        which = lax.rem(here + quarters - distance, quarters)
        base = here * slot_count
        bag_size = width // GROUP
        key_rows = lax.broadcasted_iota(jnp.int32, (highs * GROUP, width), 0).astype(jnp.bfloat16)
        low_rows = lax.broadcasted_iota(jnp.int32, (LOW, width), 0).astype(jnp.bfloat16)
        lane = lax.broadcasted_iota(jnp.int32, (blocks, width), 1)
        bag_lane = lane // bag_size
        place_lane = lane - bag_lane * bag_size
        bag_rows = lax.broadcasted_iota(jnp.int32, (rows_per, width), 0) & (GROUP - 1)
        bag_lanes = lax.broadcasted_iota(jnp.int32, (rows_per, width), 1) // bag_size
        widen = jnp.where(bag_rows == bag_lanes, 1.0, 0.0).astype(jnp.bfloat16)
        row_block = lax.broadcasted_iota(jnp.int32, (blocks, rows_per), 1) // GROUP
        own_block = row_block == lax.broadcasted_iota(jnp.int32, (blocks, rows_per), 0)
        one = jnp.ones((), jnp.bfloat16)
        zero = jnp.zeros((), jnp.bfloat16)

        def owner_step(owner, carry):
            slots = lookups_ref[owner, which] - base
            bag_lengths = lengths_ref[pl.ds(owner * quarters + which, 1), :].astype(jnp.float32)
            bag_lengths = jnp.where(own_block, bag_lengths, 0.0).astype(jnp.bfloat16)
            used = jnp.dot(bag_lengths, widen, preferred_element_type=jnp.float32)
            used = used.astype(jnp.int32)
            usable = (place_lane < used) & (slots >= 0) & (slots < slot_count)
            keys = jnp.where(usable, (slots >> LOW_BITS) * GROUP + bag_lane, -1)
            lows = slots & (LOW - 1)
            keys = keys.astype(jnp.float32).astype(jnp.bfloat16)
            lows = lows.astype(jnp.float32).astype(jnp.bfloat16)
            for block in range(blocks):
                hot_key = jnp.where(key_rows == keys[block : block + 1, :], one, zero)
                hot_low = jnp.where(low_rows == lows[block : block + 1, :], one, zero)
                counts = lax.dot_general(
                    hot_key.astype(jnp.float8_e4m3fn),
                    hot_low.astype(jnp.float8_e4m3fn),
                    (((1,), (1,)), ((), ())),
                    preferred_element_type=jnp.float32,
                )
                start = pl.multiple_of(owner * rows_per + block * GROUP, GROUP)
                counts_ref[:, pl.ds(start, GROUP), :] = counts.astype(jnp.bfloat16).reshape(
                    highs, GROUP, LOW
                )
            return carry

        lax.fori_loop(0, owners, owner_step, 0, unroll=2)
        tile = min(total, 512)

        def tile_step(index, carry):
            start = pl.multiple_of(index * tile, tile)
            acc = jnp.zeros((tile, emb), jnp.float32)
            for high in range(highs):
                acc = acc + jnp.dot(
                    counts_ref[high, pl.ds(start, tile), :],
                    table_ref[high * LOW : (high + 1) * LOW, :],
                    preferred_element_type=jnp.float32,
                )
            out_ref[pl.ds(start, tile), :] = acc.astype(out_ref.dtype)
            return carry

        lax.fori_loop(0, total // tile, tile_step, 0)

    return pl.pallas_call(
        kernel,
        out_shape=jax.ShapeDtypeStruct((total, emb), jnp.bfloat16 if distance else jnp.float32),
        scratch_shapes=[pltpu.VMEM((highs, total, LOW), jnp.bfloat16)],
        cost_estimate=pl.CostEstimate(
            flops=4 * total * slot_count * emb, bytes_accessed=2 * total * emb, transcendentals=0
        ),
        name="pool_quarter",
    )(lookups, lengths, cache_table)


def section_rows(counts, rows, slots, slot_count):
    count = counts.shape[0]
    held, emb = rows.shape
    spans = SEND_CAP // emb

    def kernel(counts_ref, rows_ref, slots_ref, *out_refs):
        here = lax.axis_index("narrow")
        row_ids = lax.broadcasted_iota(jnp.int32, (SEND_CAP, held), 0)
        places = lax.broadcasted_iota(jnp.int32, (SEND_CAP, held), 1)
        live_lanes = lax.broadcasted_iota(jnp.int32, (1, SEND_CAP), 1)
        for distance, out_ref in enumerate(out_refs):
            owner = lax.rem(here + count - distance, count)
            start = jnp.int32(0)
            for other in range(count):
                start = start + jnp.where(other < owner, counts_ref[other], 0)
            live = counts_ref[owner]
            source = jnp.where(row_ids < live, row_ids + start, -1)
            hot = jnp.where(source == places, 1.0, 0.0).astype(jnp.bfloat16)
            picked = jnp.dot(hot, rows_ref[...], preferred_element_type=jnp.float32)
            out_ref[:SEND_CAP, :] = picked.astype(jnp.bfloat16)
            local = slots_ref[...] - owner * slot_count
            digits = jnp.concatenate([local >> LOW_BITS, local & (LOW - 1)] * 4, axis=0)
            digits = digits.astype(jnp.float32).astype(jnp.bfloat16)
            moved = lax.dot_general(
                digits, hot, (((1,), (1,)), ((), ())), preferred_element_type=jnp.float32
            )
            high = jnp.where(live_lanes < live, moved[0:1, :], -1.0)
            low = moved[1:2, :]
            tail = [high[:, span * emb : (span + 1) * emb] for span in range(spans)]
            tail += [low[:, span * emb : (span + 1) * emb] for span in range(spans)]
            tail.append(jnp.zeros((GROUP - 2 * spans, emb), jnp.float32))
            out_ref[SEND_CAP:, :] = jnp.concatenate(tail, axis=0).astype(jnp.bfloat16)

    smem = pl.BlockSpec(memory_space=pltpu.SMEM)
    vmem = pl.BlockSpec(memory_space=pltpu.VMEM)
    return pl.pallas_call(
        kernel,
        out_shape=tuple(
            jax.ShapeDtypeStruct((SEND_CAP + GROUP, emb), jnp.bfloat16) for _ in range(count)
        ),
        in_specs=[smem, vmem, vmem],
        out_specs=tuple(vmem for _ in range(count)),
        cost_estimate=pl.CostEstimate(
            flops=2 * count * SEND_CAP * held * emb,
            bytes_accessed=4 * held * emb,
            transcendentals=0,
        ),
        name="section_rows",
    )(counts, rows, slots.reshape(1, held))


def place_rows(pieces, cache_table):
    slot_count, emb = cache_table.shape
    spans = SEND_CAP // emb
    arrived = SEND_CAP * len(pieces)

    def kernel(*refs):
        piece_refs = refs[: len(pieces)]
        cache_ref, out_ref, rows_ref = refs[len(pieces) :]
        high, low = [], []
        for index, piece in enumerate(piece_refs):
            rows_ref[index * SEND_CAP : (index + 1) * SEND_CAP, :emb] = piece[:SEND_CAP, :]
            digits = piece[SEND_CAP:, :].astype(jnp.float32)
            high += [digits[span : span + 1, :] for span in range(spans)]
            low += [digits[spans + span : spans + span + 1, :] for span in range(spans)]
        rows_ref[:, emb:] = jnp.ones((arrived, emb), jnp.bfloat16)
        high = jnp.concatenate(high, axis=1)
        low = jnp.concatenate(low, axis=1)
        low_rows = lax.broadcasted_iota(jnp.int32, (LOW, arrived), 0).astype(jnp.bfloat16)
        one = jnp.ones((), jnp.bfloat16)
        zero = jnp.zeros((), jnp.bfloat16)

        def step(index, carry):
            start = pl.multiple_of(index * LOW, LOW)
            targets = jnp.where(high == index.astype(jnp.float32), low, -1.0).astype(jnp.bfloat16)
            hot = jnp.where(low_rows == targets, one, zero)
            placed = jnp.dot(hot, rows_ref[...], preferred_element_type=jnp.float32)
            old = cache_ref[pl.ds(start, LOW), :]
            fresh = jnp.where(placed[:, emb:] > 0.5, placed[:, :emb], old.astype(jnp.float32))
            out_ref[pl.ds(start, LOW), :] = fresh.astype(jnp.bfloat16)
            return carry

        lax.fori_loop(0, slot_count // LOW, step, 0, unroll=2)

    return pl.pallas_call(
        kernel,
        out_shape=jax.ShapeDtypeStruct((slot_count, emb), jnp.bfloat16),
        scratch_shapes=[pltpu.VMEM((arrived, 2 * emb), jnp.bfloat16)],
        cost_estimate=pl.CostEstimate(
            flops=4 * arrived * slot_count * emb,
            bytes_accessed=4 * slot_count * emb,
            transcendentals=0,
        ),
        name="place_rows",
    )(*pieces, cache_table)


def top_network(features, first_own, second_own, parts, biases, b_second, w_out):
    count = len(features)
    quarter_rows, depth = features[0].shape
    rows = count * quarter_rows
    hidden = first_own.shape[1]
    columns = second_own.shape[1]
    flat_parts, layout = [], []
    for distance, pieces in parts.items():
        for mask, array, spans in pieces:
            layout.append((distance, mask, spans))
            flat_parts.append(array)
    tile = min(hidden, 512)

    def kernel(*refs):
        feature_refs = refs[:count]
        first_ref, second_ref = refs[count : count + 2]
        part_refs = refs[count + 2 : count + 2 + len(flat_parts)]
        rest = refs[count + 2 + len(flat_parts) :]
        bias_ref, b_second_ref, w_out_ref, top_ref, logit_ref = rest[:5]
        feats, firsts, seconds, hiddens, feat_sem, sems = rest[5:]
        wide_index = lax.axis_index("wide")
        narrow_index = lax.axis_index("narrow")
        for distance, ref in enumerate(feature_refs):
            spot = lax.rem(narrow_index + distance, count) * quarter_rows
            spot = pl.multiple_of(spot, quarter_rows)
            pltpu.make_async_copy(ref, feats.at[pl.ds(spot, quarter_rows), :], feat_sem).start()

        def fetch(which, wanted):
            if wanted == 0:
                if which == 0:
                    source, target = first_ref, firsts.at[0]
                else:
                    source = second_ref
                    target = seconds.at[:hidden, :]
                pltpu.make_async_copy(source, target, sems.at[which, 0]).start()
            for (distance, mask, spans), ref in zip(layout, part_refs):
                for layer, row, height in spans:
                    if layer != which or distance != wanted:
                        continue
                    spot = pl.multiple_of((wide_index ^ mask) * height, height)
                    target = firsts.at[distance] if which == 0 else seconds
                    spot = spot + which * distance * hidden
                    pltpu.make_async_copy(
                        ref.at[row : row + height, :],
                        target.at[pl.ds(spot, height), :],
                        sems.at[which, distance],
                    ).start()

        for distance in range(count):
            fetch(0, distance)
        pltpu.make_async_copy(feats, feats, feat_sem).wait()
        for distance in range(count):
            pltpu.make_async_copy(firsts.at[distance], firsts.at[distance], sems.at[0, distance]).wait()
            fetch(1, distance)
            for start in range(0, hidden, tile):
                terms = jnp.dot(
                    feats[...],
                    firsts[distance, :, start : start + tile],
                    preferred_element_type=jnp.float32,
                )
                bias = bias_ref[distance : distance + 1, start : start + tile]
                spot = distance * hidden + start
                hiddens[:, spot : spot + tile] = jnp.maximum(terms + bias, 0.0).astype(jnp.bfloat16)
        for distance in range(count):
            block = seconds.at[distance * hidden : (distance + 1) * hidden, :]
            pltpu.make_async_copy(block, block, sems.at[1, distance]).wait()
        for start in range(0, columns, tile):
            terms = jnp.dot(
                hiddens[...], seconds[:, start : start + tile], preferred_element_type=jnp.float32
            )
            terms = jnp.maximum(terms + b_second_ref[:, start : start + tile], 0.0)
            top_ref[:, start : start + tile] = terms.astype(jnp.bfloat16)
        logit_ref[...] = lax.dot_general(
            w_out_ref[...], top_ref[...], (((1,), (1,)), ((), ())), preferred_element_type=jnp.float32
        )[:1]

    held = 2 * count * hidden * (depth + columns + rows) + 2 * rows * (depth + columns)
    room = min(held + 8 * rows * columns + (4 << 20), 60 << 20)
    anywhere = pl.BlockSpec(memory_space=pl.ANY)
    local = pl.BlockSpec(memory_space=pltpu.VMEM)
    return pl.pallas_call(
        kernel,
        out_shape=(
            jax.ShapeDtypeStruct((rows, columns), jnp.bfloat16),
            jax.ShapeDtypeStruct((1, rows), jnp.float32),
        ),
        in_specs=[anywhere] * (count + 2 + len(flat_parts)) + [local] * 3,
        out_specs=(local, local),
        scratch_shapes=[
            pltpu.VMEM((rows, depth), jnp.bfloat16),
            pltpu.VMEM((count, depth, hidden), jnp.bfloat16),
            pltpu.VMEM((count * hidden, columns), jnp.bfloat16),
            pltpu.VMEM((rows, count * hidden), jnp.bfloat16),
            pltpu.SemaphoreType.DMA,
            pltpu.SemaphoreType.DMA((2, count)),
        ],
        cost_estimate=pl.CostEstimate(
            flops=2 * rows * count * hidden * (depth + columns),
            bytes_accessed=2 * count * hidden * (depth + columns),
            transcendentals=0,
        ),
        compiler_params=pltpu.CompilerParams(vmem_limit_bytes=room),
        name="top_network",
    )(
        *features,
        first_own,
        second_own,
        *flat_parts,
        jnp.stack(biases),
        b_second.reshape(1, columns),
        jnp.broadcast_to(w_out.reshape(1, columns), (8, columns)),
    )


def after(value, *earlier):
    return lax.optimization_barrier((value,) + earlier)[0]


def spread(piece, spans, bits, wide_count, gate=None):
    if gate is not None:
        piece = after(piece, gate)
    pieces = [(0, piece)]
    for bit in bits:
        flipped = []
        for mask, array in pieces:
            flipped.append((mask ^ bit, from_flipped(array, bit, wide_count)))
        pieces = pieces + flipped
    pieces = pieces + [
        (mask ^ 1, from_flipped(array, 1, wide_count)) for mask, array in pieces
    ]
    return [(mask, array, spans) for mask, array in pieces]


def step(
    cache,
    lookup_slots,
    bag_lengths,
    miss_rows,
    miss_slots,
    holder_counts,
    w_first,
    b_first,
    w_second,
    b_second,
    w_out,
):
    wide_count = lax.axis_size("wide")
    count = lax.axis_size("narrow")
    wide_index = lax.axis_index("wide")
    narrow_index = lax.axis_index("narrow")
    cache_table = cache[0]
    slot_count, emb = cache_table.shape
    lookups = lookup_slots[0]
    lengths = bag_lengths[0]
    batch_rows, bag_size = lookups.shape
    owner_rows = batch_rows // wide_count
    quarter_rows = owner_rows // count
    columns = w_second.shape[1] // count

    bits = [1 << place for place in range(1, (wide_count - 1).bit_length())]
    first_height = w_first.shape[0] // wide_count
    second_height = w_second.shape[0] // wide_count
    first_slice = lax.dynamic_slice_in_dim(w_first, wide_index * first_height, first_height, 0)

    def slices_for(distance):
        taker = lax.rem(narrow_index + count - distance, count)
        second_slice = lax.dynamic_slice(
            w_second,
            (wide_index * second_height, taker * columns),
            (second_height, columns),
        )
        return first_slice, second_slice

    both_spans = ((0, 0, first_height), (1, first_height, second_height))

    def merged(distance, gate=None):
        message = jnp.concatenate(slices_for(distance), axis=0)
        if gate is not None:
            message = after(message, gate)
        return from_ahead(message, distance, count)

    last = count // 2
    early = [distance for distance in range(1, count) if distance != last]
    arrived_slices = {distance: merged(distance) for distance in early[:1]}

    lookups = lookups.reshape(wide_count, count, quarter_rows // GROUP, GROUP * bag_size)
    lengths = lengths.reshape(wide_count * count, quarter_rows)
    sent, pooled = [], []
    for distance in range(count - 1, -1, -1):
        own_part = pool_quarter(lookups, lengths, cache_table, distance)
        pooled.append(own_part)
        if distance:
            sent.append(from_ahead(own_part, distance, count))
    for distance in early[1:]:
        arrived_slices[distance] = merged(distance, pooled[0])
    summed = own_part.astype(jnp.float32)
    for part in sent:
        summed = summed + part.astype(jnp.float32)
    summed = summed.astype(jnp.bfloat16).reshape(wide_count, quarter_rows, emb)
    biases = [b_first] + [
        from_ahead(after(b_first, pooled[0]), distance, count) for distance in range(1, count)
    ]
    first_piece = arrived_slices[1][:first_height]
    for _ in range(2, last + 1):
        first_piece = from_ahead(after(first_piece, own_part), 1, count)
    second_piece = from_ahead(after(slices_for(last)[1], own_part), last, count)
    arrived_slices[last] = first_piece, second_piece
    arrived = lax.all_to_all(summed, "wide", split_axis=0, concat_axis=0, tiled=True)
    own_features = jnp.transpose(arrived, (1, 0, 2)).reshape(quarter_rows, wide_count * emb)
    features = [own_features] + [
        from_ahead(own_features, distance, count) for distance in range(1, count)
    ]

    sections = section_rows(
        holder_counts[0], after(miss_rows[0], own_part), miss_slots[0], slot_count
    )
    arrived_rows = [sections[0]] + [
        from_ahead(sections[distance], distance, count) for distance in range(1, count)
    ]

    parts = {
        distance: spread(
            arrived_slices[distance],
            both_spans,
            bits if place % 2 else bits[::-1],
            wide_count,
            own_part if place else pooled[0],
        )
        for place, distance in enumerate(early)
    }
    first_piece, second_piece = arrived_slices[last]
    parts[last] = spread(
        first_piece, ((0, 0, first_height),), bits, wide_count, own_features
    ) + spread(second_piece, ((1, 0, second_height),), bits[::-1], wide_count, own_features)
    own_second = lax.dynamic_slice(
        w_second,
        (0, after(narrow_index, own_part) * columns),
        (w_second.shape[0], columns),
    )
    top_hidden, logit_terms = top_network(
        features, w_first, own_second, parts, biases, b_second, w_out
    )
    shares = [logit_terms] + [
        from_ahead(logit_terms, distance, count) for distance in range(1, count)
    ]
    while len(shares) > 1:
        half = len(shares) // 2
        shares = [shares[place] + shares[place + half] for place in range(half)]
    logits = shares[0].reshape(owner_rows)

    cache_next = place_rows(arrived_rows, cache_table)[None]
    return (top_hidden, logits, cache_next)


def solution(mesh):
    return jax.shard_map(
        step,
        mesh=mesh,
        in_specs=(
            P("wide", "narrow", None),
            P("wide", None, None),
            P("wide", None),
            P("wide", "narrow", None),
            P("wide", "narrow"),
            P("wide", "narrow"),
            P(None, "narrow"),
            P("narrow"),
            P("narrow", None),
            P("narrow"),
            P("narrow"),
        ),
        out_specs=(P("wide", "narrow"), P("wide"), P("wide", "narrow", None)),
        check_vma=False,
    )
```

```python
import jax
import jax.numpy as jnp
from jax import lax
from jax.experimental import pallas as pl
from jax.experimental.pallas import tpu as pltpu
from jax.sharding import PartitionSpec as P


SEND_CAP = 512
LOW_BITS = 8
LOW = 1 << LOW_BITS
GROUP = 16


def from_ahead(value, distance, count):
    pairs = [(source, (source - distance) % count) for source in range(count)]
    return lax.ppermute(value, "narrow", pairs)


def from_flipped(value, bit, count):
    return lax.ppermute(value, "wide", [(index, index ^ bit) for index in range(count)])


def pool_quarter(lookups, lengths, cache_table, distance):
    owners, quarters, blocks, width = lookups.shape
    slot_count, emb = cache_table.shape
    highs = slot_count // LOW
    rows_per = blocks * GROUP
    total = owners * rows_per

    def kernel(lookups_ref, lengths_ref, table_ref, out_ref, counts_ref):
        here = lax.axis_index("narrow")
        which = lax.rem(here + quarters - distance, quarters)
        base = here * slot_count
        bag_size = width // GROUP
        key_rows = lax.broadcasted_iota(jnp.int32, (highs * GROUP, width), 0).astype(jnp.bfloat16)
        low_rows = lax.broadcasted_iota(jnp.int32, (LOW, width), 0).astype(jnp.bfloat16)
        lane = lax.broadcasted_iota(jnp.int32, (blocks, width), 1)
        bag_lane = lane // bag_size
        place_lane = lane - bag_lane * bag_size
        bag_rows = lax.broadcasted_iota(jnp.int32, (rows_per, width), 0) & (GROUP - 1)
        bag_lanes = lax.broadcasted_iota(jnp.int32, (rows_per, width), 1) // bag_size
        widen = jnp.where(bag_rows == bag_lanes, 1.0, 0.0).astype(jnp.bfloat16)
        row_block = lax.broadcasted_iota(jnp.int32, (blocks, rows_per), 1) // GROUP
        own_block = row_block == lax.broadcasted_iota(jnp.int32, (blocks, rows_per), 0)
        one = jnp.ones((), jnp.bfloat16)
        zero = jnp.zeros((), jnp.bfloat16)

        def owner_step(owner, carry):
            slots = lookups_ref[owner, which] - base
            bag_lengths = lengths_ref[pl.ds(owner * quarters + which, 1), :].astype(jnp.float32)
            bag_lengths = jnp.where(own_block, bag_lengths, 0.0).astype(jnp.bfloat16)
            used = jnp.dot(bag_lengths, widen, preferred_element_type=jnp.float32)
            used = used.astype(jnp.int32)
            usable = (place_lane < used) & (slots >= 0) & (slots < slot_count)
            keys = jnp.where(usable, (slots >> LOW_BITS) * GROUP + bag_lane, -1)
            lows = slots & (LOW - 1)
            keys = keys.astype(jnp.float32).astype(jnp.bfloat16)
            lows = lows.astype(jnp.float32).astype(jnp.bfloat16)
            for block in range(blocks):
                hot_key = jnp.where(key_rows == keys[block : block + 1, :], one, zero)
                hot_low = jnp.where(low_rows == lows[block : block + 1, :], one, zero)
                counts = lax.dot_general(
                    hot_key.astype(jnp.float8_e4m3fn),
                    hot_low.astype(jnp.float8_e4m3fn),
                    (((1,), (1,)), ((), ())),
                    preferred_element_type=jnp.float32,
                )
                start = pl.multiple_of(owner * rows_per + block * GROUP, GROUP)
                counts_ref[:, pl.ds(start, GROUP), :] = counts.astype(jnp.bfloat16).reshape(
                    highs, GROUP, LOW
                )
            return carry

        lax.fori_loop(0, owners, owner_step, 0, unroll=2)
        tile = min(total, 512)

        def tile_step(index, carry):
            start = pl.multiple_of(index * tile, tile)
            acc = jnp.zeros((tile, emb), jnp.float32)
            for high in range(highs):
                acc = acc + jnp.dot(
                    counts_ref[high, pl.ds(start, tile), :],
                    table_ref[high * LOW : (high + 1) * LOW, :],
                    preferred_element_type=jnp.float32,
                )
            out_ref[pl.ds(start, tile), :] = acc.astype(out_ref.dtype)
            return carry

        lax.fori_loop(0, total // tile, tile_step, 0)

    return pl.pallas_call(
        kernel,
        out_shape=jax.ShapeDtypeStruct((total, emb), jnp.bfloat16 if distance else jnp.float32),
        scratch_shapes=[pltpu.VMEM((highs, total, LOW), jnp.bfloat16)],
        cost_estimate=pl.CostEstimate(
            flops=4 * total * slot_count * emb, bytes_accessed=2 * total * emb, transcendentals=0
        ),
        name="pool_quarter",
    )(lookups, lengths, cache_table)


def section_rows(counts, rows, slots, slot_count):
    count = counts.shape[0]
    held, emb = rows.shape
    spans = SEND_CAP // emb

    def kernel(counts_ref, rows_ref, slots_ref, *out_refs):
        here = lax.axis_index("narrow")
        row_ids = lax.broadcasted_iota(jnp.int32, (SEND_CAP, held), 0)
        places = lax.broadcasted_iota(jnp.int32, (SEND_CAP, held), 1)
        live_lanes = lax.broadcasted_iota(jnp.int32, (1, SEND_CAP), 1)
        for distance, out_ref in enumerate(out_refs):
            owner = lax.rem(here + count - distance, count)
            start = jnp.int32(0)
            for other in range(count):
                start = start + jnp.where(other < owner, counts_ref[other], 0)
            live = counts_ref[owner]
            source = jnp.where(row_ids < live, row_ids + start, -1)
            hot = jnp.where(source == places, 1.0, 0.0).astype(jnp.bfloat16)
            picked = jnp.dot(hot, rows_ref[...], preferred_element_type=jnp.float32)
            out_ref[:SEND_CAP, :] = picked.astype(jnp.bfloat16)
            local = slots_ref[...] - owner * slot_count
            digits = jnp.concatenate([local >> LOW_BITS, local & (LOW - 1)] * 4, axis=0)
            digits = digits.astype(jnp.float32).astype(jnp.bfloat16)
            moved = lax.dot_general(
                digits, hot, (((1,), (1,)), ((), ())), preferred_element_type=jnp.float32
            )
            high = jnp.where(live_lanes < live, moved[0:1, :], -1.0)
            low = moved[1:2, :]
            tail = [high[:, span * emb : (span + 1) * emb] for span in range(spans)]
            tail += [low[:, span * emb : (span + 1) * emb] for span in range(spans)]
            tail.append(jnp.zeros((GROUP - 2 * spans, emb), jnp.float32))
            out_ref[SEND_CAP:, :] = jnp.concatenate(tail, axis=0).astype(jnp.bfloat16)

    smem = pl.BlockSpec(memory_space=pltpu.SMEM)
    vmem = pl.BlockSpec(memory_space=pltpu.VMEM)
    return pl.pallas_call(
        kernel,
        out_shape=tuple(
            jax.ShapeDtypeStruct((SEND_CAP + GROUP, emb), jnp.bfloat16) for _ in range(count)
        ),
        in_specs=[smem, vmem, vmem],
        out_specs=tuple(vmem for _ in range(count)),
        cost_estimate=pl.CostEstimate(
            flops=2 * count * SEND_CAP * held * emb,
            bytes_accessed=4 * held * emb,
            transcendentals=0,
        ),
        name="section_rows",
    )(counts, rows, slots.reshape(1, held))


def place_rows(pieces, cache_table):
    slot_count, emb = cache_table.shape
    spans = SEND_CAP // emb
    arrived = SEND_CAP * len(pieces)

    def kernel(*refs):
        piece_refs = refs[: len(pieces)]
        cache_ref, out_ref, rows_ref = refs[len(pieces) :]
        high, low = [], []
        for index, piece in enumerate(piece_refs):
            rows_ref[index * SEND_CAP : (index + 1) * SEND_CAP, :emb] = piece[:SEND_CAP, :]
            digits = piece[SEND_CAP:, :].astype(jnp.float32)
            high += [digits[span : span + 1, :] for span in range(spans)]
            low += [digits[spans + span : spans + span + 1, :] for span in range(spans)]
        rows_ref[:, emb:] = jnp.ones((arrived, emb), jnp.bfloat16)
        high = jnp.concatenate(high, axis=1)
        low = jnp.concatenate(low, axis=1)
        low_rows = lax.broadcasted_iota(jnp.int32, (LOW, arrived), 0).astype(jnp.bfloat16)
        one = jnp.ones((), jnp.bfloat16)
        zero = jnp.zeros((), jnp.bfloat16)

        def step(index, carry):
            start = pl.multiple_of(index * LOW, LOW)
            targets = jnp.where(high == index.astype(jnp.float32), low, -1.0).astype(jnp.bfloat16)
            hot = jnp.where(low_rows == targets, one, zero)
            placed = jnp.dot(hot, rows_ref[...], preferred_element_type=jnp.float32)
            old = cache_ref[pl.ds(start, LOW), :]
            fresh = jnp.where(placed[:, emb:] > 0.5, placed[:, :emb], old.astype(jnp.float32))
            out_ref[pl.ds(start, LOW), :] = fresh.astype(jnp.bfloat16)
            return carry

        lax.fori_loop(0, slot_count // LOW, step, 0, unroll=2)

    return pl.pallas_call(
        kernel,
        out_shape=jax.ShapeDtypeStruct((slot_count, emb), jnp.bfloat16),
        scratch_shapes=[pltpu.VMEM((arrived, 2 * emb), jnp.bfloat16)],
        cost_estimate=pl.CostEstimate(
            flops=4 * arrived * slot_count * emb,
            bytes_accessed=4 * slot_count * emb,
            transcendentals=0,
        ),
        name="place_rows",
    )(*pieces, cache_table)


def top_network(features, first_own, second_own, parts, biases, b_second, w_out):
    count = len(features)
    quarter_rows, depth = features[0].shape
    rows = count * quarter_rows
    hidden = first_own.shape[1]
    columns = second_own.shape[1]
    flat_parts, layout = [], []
    for distance, pieces in parts.items():
        for mask, array, spans in pieces:
            layout.append((distance, mask, spans))
            flat_parts.append(array)
    tile = min(hidden, 512)

    def kernel(*refs):
        feature_refs = refs[:count]
        first_ref, second_ref = refs[count : count + 2]
        part_refs = refs[count + 2 : count + 2 + len(flat_parts)]
        rest = refs[count + 2 + len(flat_parts) :]
        bias_ref, b_second_ref, w_out_ref, top_ref, logit_ref = rest[:5]
        feats, firsts, seconds, hiddens, feat_sem, sems = rest[5:]
        wide_index = lax.axis_index("wide")
        narrow_index = lax.axis_index("narrow")
        for distance, ref in enumerate(feature_refs):
            spot = lax.rem(narrow_index + distance, count) * quarter_rows
            spot = pl.multiple_of(spot, quarter_rows)
            pltpu.make_async_copy(ref, feats.at[pl.ds(spot, quarter_rows), :], feat_sem).start()

        def fetch(which, wanted):
            if wanted == 0:
                if which == 0:
                    source, target = first_ref, firsts.at[0]
                else:
                    source = second_ref
                    target = seconds.at[:hidden, :]
                pltpu.make_async_copy(source, target, sems.at[which, 0]).start()
            for (distance, mask, spans), ref in zip(layout, part_refs):
                for layer, row, height in spans:
                    if layer != which or distance != wanted:
                        continue
                    spot = pl.multiple_of((wide_index ^ mask) * height, height)
                    target = firsts.at[distance] if which == 0 else seconds
                    spot = spot + which * distance * hidden
                    pltpu.make_async_copy(
                        ref.at[row : row + height, :],
                        target.at[pl.ds(spot, height), :],
                        sems.at[which, distance],
                    ).start()

        for distance in range(count):
            fetch(0, distance)
        pltpu.make_async_copy(feats, feats, feat_sem).wait()
        for distance in range(count):
            pltpu.make_async_copy(firsts.at[distance], firsts.at[distance], sems.at[0, distance]).wait()
            fetch(1, distance)
            for start in range(0, hidden, tile):
                terms = jnp.dot(
                    feats[...],
                    firsts[distance, :, start : start + tile],
                    preferred_element_type=jnp.float32,
                )
                bias = bias_ref[distance : distance + 1, start : start + tile]
                spot = distance * hidden + start
                hiddens[:, spot : spot + tile] = jnp.maximum(terms + bias, 0.0).astype(jnp.bfloat16)
        for distance in range(count):
            block = seconds.at[distance * hidden : (distance + 1) * hidden, :]
            pltpu.make_async_copy(block, block, sems.at[1, distance]).wait()
        for start in range(0, columns, tile):
            terms = jnp.dot(
                hiddens[...], seconds[:, start : start + tile], preferred_element_type=jnp.float32
            )
            terms = jnp.maximum(terms + b_second_ref[:, start : start + tile], 0.0)
            top_ref[:, start : start + tile] = terms.astype(jnp.bfloat16)
        logit_ref[...] = lax.dot_general(
            w_out_ref[...], top_ref[...], (((1,), (1,)), ((), ())), preferred_element_type=jnp.float32
        )[:1]

    held = 2 * count * hidden * (depth + columns + rows) + 2 * rows * (depth + columns)
    room = min(held + 8 * rows * columns + (4 << 20), 60 << 20)
    anywhere = pl.BlockSpec(memory_space=pl.ANY)
    local = pl.BlockSpec(memory_space=pltpu.VMEM)
    return pl.pallas_call(
        kernel,
        out_shape=(
            jax.ShapeDtypeStruct((rows, columns), jnp.bfloat16),
            jax.ShapeDtypeStruct((1, rows), jnp.float32),
        ),
        in_specs=[anywhere] * (count + 2 + len(flat_parts)) + [local] * 3,
        out_specs=(local, local),
        scratch_shapes=[
            pltpu.VMEM((rows, depth), jnp.bfloat16),
            pltpu.VMEM((count, depth, hidden), jnp.bfloat16),
            pltpu.VMEM((count * hidden, columns), jnp.bfloat16),
            pltpu.VMEM((rows, count * hidden), jnp.bfloat16),
            pltpu.SemaphoreType.DMA,
            pltpu.SemaphoreType.DMA((2, count)),
        ],
        cost_estimate=pl.CostEstimate(
            flops=2 * rows * count * hidden * (depth + columns),
            bytes_accessed=2 * count * hidden * (depth + columns),
            transcendentals=0,
        ),
        compiler_params=pltpu.CompilerParams(vmem_limit_bytes=room),
        name="top_network",
    )(
        *features,
        first_own,
        second_own,
        *flat_parts,
        jnp.stack(biases),
        b_second.reshape(1, columns),
        jnp.broadcast_to(w_out.reshape(1, columns), (8, columns)),
    )


def after(value, *earlier):
    return lax.optimization_barrier((value,) + earlier)[0]


def spread(piece, spans, bits, wide_count, gate=None):
    if gate is not None:
        piece = after(piece, gate)
    pieces = [(0, piece)]
    for bit in bits:
        flipped = []
        for mask, array in pieces:
            flipped.append((mask ^ bit, from_flipped(array, bit, wide_count)))
        pieces = pieces + flipped
    pieces = pieces + [
        (mask ^ 1, from_flipped(array, 1, wide_count)) for mask, array in pieces
    ]
    return [(mask, array, spans) for mask, array in pieces]


def step(
    cache,
    lookup_slots,
    bag_lengths,
    miss_rows,
    miss_slots,
    holder_counts,
    w_first,
    b_first,
    w_second,
    b_second,
    w_out,
):
    wide_count = lax.axis_size("wide")
    count = lax.axis_size("narrow")
    wide_index = lax.axis_index("wide")
    narrow_index = lax.axis_index("narrow")
    cache_table = cache[0]
    slot_count, emb = cache_table.shape
    lookups = lookup_slots[0]
    lengths = bag_lengths[0]
    batch_rows, bag_size = lookups.shape
    owner_rows = batch_rows // wide_count
    quarter_rows = owner_rows // count
    columns = w_second.shape[1] // count

    bits = [1 << place for place in range(1, (wide_count - 1).bit_length())]
    first_height = w_first.shape[0] // wide_count
    second_height = w_second.shape[0] // wide_count
    first_slice = lax.dynamic_slice_in_dim(w_first, wide_index * first_height, first_height, 0)

    def slices_for(distance):
        taker = lax.rem(narrow_index + count - distance, count)
        second_slice = lax.dynamic_slice(
            w_second,
            (wide_index * second_height, taker * columns),
            (second_height, columns),
        )
        return first_slice, second_slice

    both_spans = ((0, 0, first_height), (1, first_height, second_height))

    def merged(distance, gate=None):
        message = jnp.concatenate(slices_for(distance), axis=0)
        if gate is not None:
            message = after(message, gate)
        return from_ahead(message, distance, count)

    last = count // 2
    early = [distance for distance in range(1, count) if distance != last]
    arrived_slices = {distance: merged(distance) for distance in early[:1]}

    lookups = lookups.reshape(wide_count, count, quarter_rows // GROUP, GROUP * bag_size)
    lengths = lengths.reshape(wide_count * count, quarter_rows)
    sent, pooled = [], []
    for distance in range(count - 1, -1, -1):
        own_part = pool_quarter(lookups, lengths, cache_table, distance)
        pooled.append(own_part)
        if distance:
            sent.append(from_ahead(own_part, distance, count))
    for distance in early[1:]:
        arrived_slices[distance] = merged(distance, pooled[0])
    summed = own_part.astype(jnp.float32)
    for part in sent:
        summed = summed + part.astype(jnp.float32)
    summed = summed.astype(jnp.bfloat16).reshape(wide_count, quarter_rows, emb)
    biases = [b_first] + [
        from_ahead(after(b_first, pooled[0]), distance, count) for distance in range(1, count)
    ]
    first_piece = arrived_slices[1][:first_height]
    for _ in range(2, last + 1):
        first_piece = from_ahead(after(first_piece, own_part), 1, count)
    second_piece = from_ahead(after(slices_for(last)[1], own_part), last, count)
    arrived_slices[last] = first_piece, second_piece
    arrived = lax.all_to_all(summed, "wide", split_axis=0, concat_axis=0, tiled=True)
    own_features = jnp.transpose(arrived, (1, 0, 2)).reshape(quarter_rows, wide_count * emb)
    features = {0: own_features}
    for chain, hop in ((range(1, last + 1), 1), (range(count - 1, last, -1), count - 1)):
        held = own_features
        for distance in chain:
            held = from_ahead(held, hop, count)
            features[distance] = held
    features = [features[distance] for distance in range(count)]

    sections = section_rows(
        holder_counts[0], after(miss_rows[0], own_part), miss_slots[0], slot_count
    )
    arrived_rows = [sections[0]] + [
        from_ahead(sections[distance], distance, count) for distance in range(1, count)
    ]

    parts = {
        distance: spread(
            arrived_slices[distance],
            both_spans,
            bits if place % 2 else bits[::-1],
            wide_count,
            own_part if place else pooled[0],
        )
        for place, distance in enumerate(early)
    }
    first_piece, second_piece = arrived_slices[last]
    parts[last] = spread(
        first_piece, ((0, 0, first_height),), bits[::-1], wide_count, own_features
    ) + spread(second_piece, ((1, 0, second_height),), bits[::-1], wide_count, own_features)
    own_second = lax.dynamic_slice(
        w_second,
        (0, after(narrow_index, own_part) * columns),
        (w_second.shape[0], columns),
    )
    top_hidden, logit_terms = top_network(
        features, w_first, own_second, parts, biases, b_second, w_out
    )
    shares = [logit_terms] + [
        from_ahead(logit_terms, distance, count) for distance in range(1, count)
    ]
    while len(shares) > 1:
        half = len(shares) // 2
        shares = [shares[place] + shares[place + half] for place in range(half)]
    logits = shares[0].reshape(owner_rows)

    cache_next = place_rows(arrived_rows, cache_table)[None]
    return (top_hidden, logits, cache_next)


def solution(mesh):
    return jax.shard_map(
        step,
        mesh=mesh,
        in_specs=(
            P("wide", "narrow", None),
            P("wide", None, None),
            P("wide", None),
            P("wide", "narrow", None),
            P("wide", "narrow"),
            P("wide", "narrow"),
            P(None, "narrow"),
            P("narrow"),
            P("narrow", None),
            P("narrow"),
            P("narrow"),
        ),
        out_specs=(P("wide", "narrow"), P("wide"), P("wide", "narrow", None)),
        check_vma=False,
    )
```

```python
import jax
import jax.numpy as jnp
from jax import lax
from jax.experimental import pallas as pl
from jax.experimental.pallas import tpu as pltpu
from jax.sharding import PartitionSpec as P


SEND_CAP = 512
LOW_BITS = 8
LOW = 1 << LOW_BITS
GROUP = 16


def from_ahead(value, distance, count):
    pairs = [(source, (source - distance) % count) for source in range(count)]
    return lax.ppermute(value, "narrow", pairs)


def from_flipped(value, bit, count):
    return lax.ppermute(value, "wide", [(index, index ^ bit) for index in range(count)])


def pool_quarter(lookups, lengths, cache_table, distance):
    owners, quarters, blocks, width = lookups.shape
    slot_count, emb = cache_table.shape
    highs = slot_count // LOW
    rows_per = blocks * GROUP
    total = owners * rows_per

    def kernel(lookups_ref, lengths_ref, table_ref, out_ref, counts_ref):
        here = lax.axis_index("narrow")
        which = lax.rem(here + quarters - distance, quarters)
        base = here * slot_count
        bag_size = width // GROUP
        key_rows = lax.broadcasted_iota(jnp.int32, (highs * GROUP, width), 0).astype(jnp.bfloat16)
        low_rows = lax.broadcasted_iota(jnp.int32, (LOW, width), 0).astype(jnp.bfloat16)
        lane = lax.broadcasted_iota(jnp.int32, (blocks, width), 1)
        bag_lane = lane // bag_size
        place_lane = lane - bag_lane * bag_size
        bag_rows = lax.broadcasted_iota(jnp.int32, (rows_per, width), 0) & (GROUP - 1)
        bag_lanes = lax.broadcasted_iota(jnp.int32, (rows_per, width), 1) // bag_size
        widen = jnp.where(bag_rows == bag_lanes, 1.0, 0.0).astype(jnp.bfloat16)
        row_block = lax.broadcasted_iota(jnp.int32, (blocks, rows_per), 1) // GROUP
        own_block = row_block == lax.broadcasted_iota(jnp.int32, (blocks, rows_per), 0)
        one = jnp.ones((), jnp.bfloat16)
        zero = jnp.zeros((), jnp.bfloat16)

        def owner_step(owner, carry):
            slots = lookups_ref[owner, which] - base
            bag_lengths = lengths_ref[pl.ds(owner * quarters + which, 1), :].astype(jnp.float32)
            bag_lengths = jnp.where(own_block, bag_lengths, 0.0).astype(jnp.bfloat16)
            used = jnp.dot(bag_lengths, widen, preferred_element_type=jnp.float32)
            used = used.astype(jnp.int32)
            usable = (place_lane < used) & (slots >= 0) & (slots < slot_count)
            keys = jnp.where(usable, (slots >> LOW_BITS) * GROUP + bag_lane, -1)
            lows = slots & (LOW - 1)
            keys = keys.astype(jnp.float32).astype(jnp.bfloat16)
            lows = lows.astype(jnp.float32).astype(jnp.bfloat16)
            for block in range(blocks):
                hot_key = jnp.where(key_rows == keys[block : block + 1, :], one, zero)
                hot_low = jnp.where(low_rows == lows[block : block + 1, :], one, zero)
                counts = lax.dot_general(
                    hot_key.astype(jnp.float8_e4m3fn),
                    hot_low.astype(jnp.float8_e4m3fn),
                    (((1,), (1,)), ((), ())),
                    preferred_element_type=jnp.float32,
                )
                start = pl.multiple_of(owner * rows_per + block * GROUP, GROUP)
                counts_ref[:, pl.ds(start, GROUP), :] = counts.astype(jnp.bfloat16).reshape(
                    highs, GROUP, LOW
                )
            return carry

        lax.fori_loop(0, owners, owner_step, 0, unroll=2)
        tile = min(total, 512)

        def tile_step(index, carry):
            start = pl.multiple_of(index * tile, tile)
            acc = jnp.zeros((tile, emb), jnp.float32)
            for high in range(highs):
                acc = acc + jnp.dot(
                    counts_ref[high, pl.ds(start, tile), :],
                    table_ref[high * LOW : (high + 1) * LOW, :],
                    preferred_element_type=jnp.float32,
                )
            out_ref[pl.ds(start, tile), :] = acc.astype(out_ref.dtype)
            return carry

        lax.fori_loop(0, total // tile, tile_step, 0)

    return pl.pallas_call(
        kernel,
        out_shape=jax.ShapeDtypeStruct((total, emb), jnp.bfloat16 if distance else jnp.float32),
        scratch_shapes=[pltpu.VMEM((highs, total, LOW), jnp.bfloat16)],
        cost_estimate=pl.CostEstimate(
            flops=4 * total * slot_count * emb, bytes_accessed=2 * total * emb, transcendentals=0
        ),
        name="pool_quarter",
    )(lookups, lengths, cache_table)


def section_rows(counts, rows, slots, slot_count):
    count = counts.shape[0]
    held, emb = rows.shape
    spans = SEND_CAP // emb

    def kernel(counts_ref, rows_ref, slots_ref, *out_refs):
        here = lax.axis_index("narrow")
        row_ids = lax.broadcasted_iota(jnp.int32, (SEND_CAP, held), 0)
        places = lax.broadcasted_iota(jnp.int32, (SEND_CAP, held), 1)
        live_lanes = lax.broadcasted_iota(jnp.int32, (1, SEND_CAP), 1)
        for distance, out_ref in enumerate(out_refs):
            owner = lax.rem(here + count - distance, count)
            start = jnp.int32(0)
            for other in range(count):
                start = start + jnp.where(other < owner, counts_ref[other], 0)
            live = counts_ref[owner]
            source = jnp.where(row_ids < live, row_ids + start, -1)
            hot = jnp.where(source == places, 1.0, 0.0).astype(jnp.bfloat16)
            picked = jnp.dot(hot, rows_ref[...], preferred_element_type=jnp.float32)
            out_ref[:SEND_CAP, :] = picked.astype(jnp.bfloat16)
            local = slots_ref[...] - owner * slot_count
            digits = jnp.concatenate([local >> LOW_BITS, local & (LOW - 1)] * 4, axis=0)
            digits = digits.astype(jnp.float32).astype(jnp.bfloat16)
            moved = lax.dot_general(
                digits, hot, (((1,), (1,)), ((), ())), preferred_element_type=jnp.float32
            )
            high = jnp.where(live_lanes < live, moved[0:1, :], -1.0)
            low = moved[1:2, :]
            tail = [high[:, span * emb : (span + 1) * emb] for span in range(spans)]
            tail += [low[:, span * emb : (span + 1) * emb] for span in range(spans)]
            tail.append(jnp.zeros((GROUP - 2 * spans, emb), jnp.float32))
            out_ref[SEND_CAP:, :] = jnp.concatenate(tail, axis=0).astype(jnp.bfloat16)

    smem = pl.BlockSpec(memory_space=pltpu.SMEM)
    vmem = pl.BlockSpec(memory_space=pltpu.VMEM)
    return pl.pallas_call(
        kernel,
        out_shape=tuple(
            jax.ShapeDtypeStruct((SEND_CAP + GROUP, emb), jnp.bfloat16) for _ in range(count)
        ),
        in_specs=[smem, vmem, vmem],
        out_specs=tuple(vmem for _ in range(count)),
        cost_estimate=pl.CostEstimate(
            flops=2 * count * SEND_CAP * held * emb,
            bytes_accessed=4 * held * emb,
            transcendentals=0,
        ),
        name="section_rows",
    )(counts, rows, slots.reshape(1, held))


def place_rows(pieces, cache_table):
    slot_count, emb = cache_table.shape
    spans = SEND_CAP // emb
    arrived = SEND_CAP * len(pieces)

    def kernel(*refs):
        piece_refs = refs[: len(pieces)]
        cache_ref, out_ref, rows_ref = refs[len(pieces) :]
        high, low = [], []
        for index, piece in enumerate(piece_refs):
            rows_ref[index * SEND_CAP : (index + 1) * SEND_CAP, :emb] = piece[:SEND_CAP, :]
            digits = piece[SEND_CAP:, :].astype(jnp.float32)
            high += [digits[span : span + 1, :] for span in range(spans)]
            low += [digits[spans + span : spans + span + 1, :] for span in range(spans)]
        rows_ref[:, emb:] = jnp.ones((arrived, emb), jnp.bfloat16)
        high = jnp.concatenate(high, axis=1)
        low = jnp.concatenate(low, axis=1)
        low_rows = lax.broadcasted_iota(jnp.int32, (LOW, arrived), 0).astype(jnp.bfloat16)
        one = jnp.ones((), jnp.bfloat16)
        zero = jnp.zeros((), jnp.bfloat16)

        def step(index, carry):
            start = pl.multiple_of(index * LOW, LOW)
            targets = jnp.where(high == index.astype(jnp.float32), low, -1.0).astype(jnp.bfloat16)
            hot = jnp.where(low_rows == targets, one, zero)
            placed = jnp.dot(hot, rows_ref[...], preferred_element_type=jnp.float32)
            old = cache_ref[pl.ds(start, LOW), :]
            fresh = jnp.where(placed[:, emb:] > 0.5, placed[:, :emb], old.astype(jnp.float32))
            out_ref[pl.ds(start, LOW), :] = fresh.astype(jnp.bfloat16)
            return carry

        lax.fori_loop(0, slot_count // LOW, step, 0, unroll=2)

    return pl.pallas_call(
        kernel,
        out_shape=jax.ShapeDtypeStruct((slot_count, emb), jnp.bfloat16),
        scratch_shapes=[pltpu.VMEM((arrived, 2 * emb), jnp.bfloat16)],
        cost_estimate=pl.CostEstimate(
            flops=4 * arrived * slot_count * emb,
            bytes_accessed=4 * slot_count * emb,
            transcendentals=0,
        ),
        name="place_rows",
    )(*pieces, cache_table)


def top_network(features, first_own, second_own, parts, biases, b_second, w_out):
    count = len(features)
    quarter_rows, depth = features[0].shape
    rows = count * quarter_rows
    hidden = first_own.shape[1]
    columns = second_own.shape[1]
    flat_parts, layout = [], []
    for distance, pieces in parts.items():
        for mask, array, spans in pieces:
            layout.append((distance, mask, spans))
            flat_parts.append(array)
    tile = min(hidden, 512)

    def kernel(*refs):
        feature_refs = refs[:count]
        first_ref, second_ref = refs[count : count + 2]
        part_refs = refs[count + 2 : count + 2 + len(flat_parts)]
        rest = refs[count + 2 + len(flat_parts) :]
        bias_ref, b_second_ref, w_out_ref, top_ref, logit_ref = rest[:5]
        feats, firsts, seconds, hiddens, feat_sem, sems = rest[5:]
        wide_index = lax.axis_index("wide")
        narrow_index = lax.axis_index("narrow")
        for distance, ref in enumerate(feature_refs):
            spot = lax.rem(narrow_index + distance, count) * quarter_rows
            spot = pl.multiple_of(spot, quarter_rows)
            pltpu.make_async_copy(ref, feats.at[pl.ds(spot, quarter_rows), :], feat_sem).start()

        def fetch(which, wanted):
            if wanted == 0:
                if which == 0:
                    source, target = first_ref, firsts.at[0]
                else:
                    source = second_ref
                    target = seconds.at[:hidden, :]
                pltpu.make_async_copy(source, target, sems.at[which, 0]).start()
            for (distance, mask, spans), ref in zip(layout, part_refs):
                for layer, row, height in spans:
                    if layer != which or distance != wanted:
                        continue
                    spot = pl.multiple_of((wide_index ^ mask) * height, height)
                    target = firsts.at[distance] if which == 0 else seconds
                    spot = spot + which * distance * hidden
                    pltpu.make_async_copy(
                        ref.at[row : row + height, :],
                        target.at[pl.ds(spot, height), :],
                        sems.at[which, distance],
                    ).start()

        for distance in range(count):
            fetch(0, distance)
        pltpu.make_async_copy(feats, feats, feat_sem).wait()
        for distance in range(count):
            pltpu.make_async_copy(firsts.at[distance], firsts.at[distance], sems.at[0, distance]).wait()
            fetch(1, distance)
            for start in range(0, hidden, tile):
                terms = jnp.dot(
                    feats[...],
                    firsts[distance, :, start : start + tile],
                    preferred_element_type=jnp.float32,
                )
                bias = bias_ref[distance : distance + 1, start : start + tile]
                spot = distance * hidden + start
                hiddens[:, spot : spot + tile] = jnp.maximum(terms + bias, 0.0).astype(jnp.bfloat16)
        for distance in range(count):
            block = seconds.at[distance * hidden : (distance + 1) * hidden, :]
            pltpu.make_async_copy(block, block, sems.at[1, distance]).wait()
        for start in range(0, columns, tile):
            terms = jnp.dot(
                hiddens[...], seconds[:, start : start + tile], preferred_element_type=jnp.float32
            )
            terms = jnp.maximum(terms + b_second_ref[:, start : start + tile], 0.0)
            top_ref[:, start : start + tile] = terms.astype(jnp.bfloat16)
        logit_ref[...] = lax.dot_general(
            w_out_ref[...], top_ref[...], (((1,), (1,)), ((), ())), preferred_element_type=jnp.float32
        )[:1]

    held = 2 * count * hidden * (depth + columns + rows) + 2 * rows * (depth + columns)
    room = min(held + 8 * rows * columns + (4 << 20), 60 << 20)
    anywhere = pl.BlockSpec(memory_space=pl.ANY)
    local = pl.BlockSpec(memory_space=pltpu.VMEM)
    return pl.pallas_call(
        kernel,
        out_shape=(
            jax.ShapeDtypeStruct((rows, columns), jnp.bfloat16),
            jax.ShapeDtypeStruct((1, rows), jnp.float32),
        ),
        in_specs=[anywhere] * (count + 2 + len(flat_parts)) + [local] * 3,
        out_specs=(local, local),
        scratch_shapes=[
            pltpu.VMEM((rows, depth), jnp.bfloat16),
            pltpu.VMEM((count, depth, hidden), jnp.bfloat16),
            pltpu.VMEM((count * hidden, columns), jnp.bfloat16),
            pltpu.VMEM((rows, count * hidden), jnp.bfloat16),
            pltpu.SemaphoreType.DMA,
            pltpu.SemaphoreType.DMA((2, count)),
        ],
        cost_estimate=pl.CostEstimate(
            flops=2 * rows * count * hidden * (depth + columns),
            bytes_accessed=2 * count * hidden * (depth + columns),
            transcendentals=0,
        ),
        compiler_params=pltpu.CompilerParams(vmem_limit_bytes=room),
        name="top_network",
    )(
        *features,
        first_own,
        second_own,
        *flat_parts,
        jnp.stack(biases),
        b_second.reshape(1, columns),
        jnp.broadcast_to(w_out.reshape(1, columns), (8, columns)),
    )


def after(value, *earlier):
    return lax.optimization_barrier((value,) + earlier)[0]


def spread(piece, spans, bits, wide_count, gate=None):
    if gate is not None:
        piece = after(piece, gate)
    pieces = [(0, piece)]
    for bit in bits:
        flipped = []
        for mask, array in pieces:
            flipped.append((mask ^ bit, from_flipped(array, bit, wide_count)))
        pieces = pieces + flipped
    others = []
    for mask, array in pieces:
        others.append((mask ^ 1, from_flipped(array, 1, wide_count)))
    pieces = pieces + others
    return [(mask, array, spans) for mask, array in pieces]


def step(
    cache,
    lookup_slots,
    bag_lengths,
    miss_rows,
    miss_slots,
    holder_counts,
    w_first,
    b_first,
    w_second,
    b_second,
    w_out,
):
    wide_count = lax.axis_size("wide")
    count = lax.axis_size("narrow")
    wide_index = lax.axis_index("wide")
    narrow_index = lax.axis_index("narrow")
    cache_table = cache[0]
    slot_count, emb = cache_table.shape
    lookups = lookup_slots[0]
    lengths = bag_lengths[0]
    batch_rows, bag_size = lookups.shape
    owner_rows = batch_rows // wide_count
    quarter_rows = owner_rows // count
    columns = w_second.shape[1] // count

    bits = [1 << place for place in range(1, (wide_count - 1).bit_length())]
    first_height = w_first.shape[0] // wide_count
    second_height = w_second.shape[0] // wide_count
    first_slice = lax.dynamic_slice_in_dim(w_first, wide_index * first_height, first_height, 0)

    def slices_for(distance):
        taker = lax.rem(narrow_index + count - distance, count)
        second_slice = lax.dynamic_slice(
            w_second,
            (wide_index * second_height, taker * columns),
            (second_height, columns),
        )
        return first_slice, second_slice

    both_spans = ((0, 0, first_height), (1, first_height, second_height))

    def merged(distance, gate=None):
        message = jnp.concatenate(slices_for(distance), axis=0)
        if gate is not None:
            message = after(message, gate)
        return from_ahead(message, distance, count)

    last = count // 2
    early = [distance for distance in range(1, count) if distance != last]
    arrived_slices = {distance: merged(distance) for distance in early[:1]}

    lookups = lookups.reshape(wide_count, count, quarter_rows // GROUP, GROUP * bag_size)
    lengths = lengths.reshape(wide_count * count, quarter_rows)
    sent, pooled = [], []
    for distance in range(count - 1, -1, -1):
        own_part = pool_quarter(lookups, lengths, cache_table, distance)
        pooled.append(own_part)
        if distance:
            sent.append(from_ahead(own_part, distance, count))
    for distance in early[1:]:
        arrived_slices[distance] = merged(distance, pooled[0])
    summed = own_part.astype(jnp.float32)
    for part in sent:
        summed = summed + part.astype(jnp.float32)
    summed = summed.astype(jnp.bfloat16).reshape(wide_count, quarter_rows, emb)
    biases = [b_first] + [
        from_ahead(after(b_first, pooled[0]), distance, count) for distance in range(1, count)
    ]
    first_piece = arrived_slices[1][:first_height]
    for _ in range(2, last + 1):
        first_piece = from_ahead(after(first_piece, own_part), 1, count)
    second_piece = from_ahead(after(slices_for(last)[1], own_part), last, count)
    arrived_slices[last] = first_piece, second_piece
    arrived = lax.all_to_all(summed, "wide", split_axis=0, concat_axis=0, tiled=True)
    own_features = jnp.transpose(arrived, (1, 0, 2)).reshape(quarter_rows, wide_count * emb)
    features = {0: own_features}
    for chain, hop in ((range(1, last + 1), 1), (range(count - 1, last, -1), count - 1)):
        held = own_features
        for distance in chain:
            held = from_ahead(held, hop, count)
            features[distance] = held
    features = [features[distance] for distance in range(count)]

    sections = section_rows(
        holder_counts[0], after(miss_rows[0], own_part), miss_slots[0], slot_count
    )
    arrived_rows = [sections[0]] + [
        from_ahead(sections[distance], distance, count) for distance in range(1, count)
    ]

    parts = {
        distance: spread(
            arrived_slices[distance],
            both_spans,
            bits if place % 2 else bits[::-1],
            wide_count,
            own_part if place else pooled[0],
        )
        for place, distance in enumerate(early)
    }
    first_piece, second_piece = arrived_slices[last]
    parts[last] = spread(
        first_piece, ((0, 0, first_height),), bits[::-1], wide_count, own_features
    ) + spread(second_piece, ((1, 0, second_height),), bits[::-1], wide_count, own_features)
    own_second = lax.dynamic_slice(
        w_second,
        (0, after(narrow_index, own_part) * columns),
        (w_second.shape[0], columns),
    )
    top_hidden, logit_terms = top_network(
        features, w_first, own_second, parts, biases, b_second, w_out
    )
    shares = [logit_terms] + [
        from_ahead(logit_terms, distance, count) for distance in range(1, count)
    ]
    while len(shares) > 1:
        half = len(shares) // 2
        shares = [shares[place] + shares[place + half] for place in range(half)]
    logits = shares[0].reshape(owner_rows)

    cache_next = place_rows(arrived_rows, cache_table)[None]
    return (top_hidden, logits, cache_next)


def solution(mesh):
    return jax.shard_map(
        step,
        mesh=mesh,
        in_specs=(
            P("wide", "narrow", None),
            P("wide", None, None),
            P("wide", None),
            P("wide", "narrow", None),
            P("wide", "narrow"),
            P("wide", "narrow"),
            P(None, "narrow"),
            P("narrow"),
            P("narrow", None),
            P("narrow"),
            P("narrow"),
        ),
        out_specs=(P("wide", "narrow"), P("wide"), P("wide", "narrow", None)),
        check_vma=False,
    )
```
